512 devices in a mesh: blk: 64 (over y, z_lo, core), lay: 8 (over z_hi, x).
Axes of the slice: x: 4, y: 4, z: 16 (z_hi: 2, z_lo: 8; z = z_hi * 8 + z_lo), core: 2. Of those that a mesh axis runs over, the one named last changes fastest.
Arguments:
- spectra: bfloat16 [2, 256, 4, 1024], P(None, 'blk'), may hold values from -6 to 6
- model_corr: bfloat16 [64, 32, 4, 4, 1024], P('blk', 'lay'), may hold values from -6 to 6
- window_start: int32 [64, 32], P('blk', 'lay'), may hold values from 0 to 511
- window_end: int32 [64, 32], P('blk', 'lay'), may hold values from 513 to 1024
- station_slot: int32 [64, 4], P('blk'), may hold values from 0 to 3, each once within a row
Outputs:
- adjoint: float32 [2, 256, 4, 1024], P(None, 'blk', None, 'lay')
The draws below stay inside these ranges and needn't reach their ends.
Inputs may be any that keep to these rules, and one draw needn't show every extreme that they name: `station_slot`: each row lists every number from 0 to 3 once. `window_start`: every taper starts before the middle lag sample. `window_end`: every taper ends after the middle lag sample.
All inputs are finite; a program needn't handle non-finite values.
Results may differ from the reference program's by a relative error of at most 0.0022.
Values may be sent and summed in bfloat16 or wider, within the bound.
A program may use at most 64 MiB of HBM per device.

```python
import functools
import math
import jax
import jax.numpy as jnp
from jax import lax

STA = 4
WIN = 4
FREQ = 1024
LAGS = 1024
NBLK = 64
OFFSETS = 32
NSTA = 256


def plant(array, stream_key, low, top_value):
    spot = [jax.random.randint(jax.random.fold_in(stream_key, axis), (), 0, length) for axis, length in enumerate(array.shape)]
    main_axis = array.shape.index(max(array.shape))
    beside = spot[:main_axis] + [(spot[main_axis] + 1) % array.shape[main_axis]] + spot[main_axis + 1:]
    return array.at[tuple(spot)].set(low).at[tuple(beside)].set(top_value)


def levels(own_key, shape, pieces, least, high):
    def one(position, blocks):
        heights = jax.random.uniform(jax.random.fold_in(jax.random.fold_in(own_key, 6), position), (blocks,), jnp.float32, least / len(pieces), high / len(pieces))
        return jnp.repeat(jnp.exp(heights), shape[position] // blocks).reshape((-1,) + (1,) * (len(shape) - position - 1))

    level = one(*pieces[0])
    for cut in pieces[1:]:
        level = level * one(*cut)
    return level


def noise(rng, shape, deviation, most, shards=(), kind=jnp.bfloat16):
    values = jax.random.normal(rng, shape, jnp.float32) * deviation
    if len(shards) > 0:
        values = levels(rng, shape, shards, -0.22, 0.18) * values
    return jnp.clip(values, min=-most, max=most).astype(kind)


def setup_inputs(seed: int = 0) -> dict:
    streams_of = jax.random.split(jax.random.key(seed), 6)
    return {
        "spectra": noise(streams_of[0], (2, NSTA, WIN, FREQ), 1.0, 6.0, ((1, 64),)),
        "model_corr": noise(streams_of[1], (NBLK, OFFSETS, STA, STA, LAGS), 1.0, 6.0, ((0, 64), (1, 8))),
        "window_start": plant(jax.random.randint(streams_of[2], (NBLK, OFFSETS), 0, LAGS // 2), jax.random.fold_in(streams_of[2], 1), 0, (LAGS // 2) - 1).astype(jnp.int32),
        "window_end": plant(jax.random.randint(streams_of[3], (NBLK, OFFSETS), LAGS // 2 + 1, LAGS + 1), jax.random.fold_in(streams_of[3], 1), LAGS // 2 + 1, LAGS).astype(jnp.int32),
        "station_slot": jax.vmap(lambda own: jax.random.permutation(own, STA))(jax.random.split(streams_of[4], NBLK)).reshape((NBLK, STA)).astype(jnp.int32),
    }


def lag_table(freq_count, lag_count, window_count):
    freq_index = jnp.arange(freq_count, dtype=jnp.int32)
    lag_index = jnp.arange(lag_count, dtype=jnp.int32) - lag_count // 2
    phase_index = freq_index[:, None] * lag_index[None, :] % (2 * freq_count)
    angle = phase_index.astype(jnp.float32) * (math.pi / freq_count)
    factor = 1.0 / math.sqrt(2.0 * freq_count * window_count)
    cosine = (jnp.cos(angle) * factor).astype(jnp.bfloat16)
    sine = (-jnp.sin(angle) * factor).astype(jnp.bfloat16)
    return jnp.concatenate([cosine, sine], axis=0)

def reference(spectra, model_corr, window_start, window_end, station_slot):
    blocked = spectra.reshape(2, NBLK, STA, WIN, FREQ)
    slot_index = jnp.broadcast_to(station_slot.astype(jnp.int32)[None, :, :, None, None], blocked.shape)
    ordered = jnp.take_along_axis(blocked, slot_index, axis=2)
    table = lag_table(FREQ, LAGS, WIN).astype(jnp.float32)
    lag_pos = jnp.arange(LAGS, dtype=jnp.int32)
    station_pos = jnp.arange(STA, dtype=jnp.int32)
    diagonal = station_pos[:, None] == station_pos[None, :]
    einsum_high = functools.partial(jnp.einsum, precision=lax.Precision.HIGHEST)
    first = ordered.astype(jnp.float32)

    def one_offset(summed, offset):
        second = jnp.roll(ordered, -offset, axis=1).astype(jnp.float32)
        cross_re = einsum_high('bitf,bjtf->bijf', first[0], second[0]) + einsum_high('bitf,bjtf->bijf', first[1], second[1])
        cross_im = einsum_high('bitf,bjtf->bijf', first[1], second[0]) - einsum_high('bitf,bjtf->bijf', first[0], second[1])
        cross = jnp.concatenate([cross_re.astype(jnp.bfloat16), cross_im.astype(jnp.bfloat16)], axis=3)
        cross = lax.optimization_barrier(cross).astype(jnp.float32)
        lagged = jnp.dot(cross.reshape(-1, 2 * FREQ), table, precision=lax.Precision.HIGHEST)
        lagged = lagged.reshape(NBLK, STA, STA, LAGS)
        model = lax.dynamic_index_in_dim(model_corr, offset, 1, keepdims=False).astype(jnp.float32)
        starts = lax.dynamic_index_in_dim(window_start, offset, 1, keepdims=False)
        ends = lax.dynamic_index_in_dim(window_end, offset, 1, keepdims=False)
        inside = (lag_pos[None, :] >= starts[:, None]) & (lag_pos[None, :] < ends[:, None])
        paired = jnp.logical_not((offset == 0) & diagonal)
        keep = inside[:, None, None, :] & paired[None, :, :, None]
        misfit = jnp.where(keep, lagged - model, 0.0).astype(jnp.bfloat16)
        misfit = lax.optimization_barrier(misfit).astype(jnp.float32)
        response = jnp.dot(misfit.reshape(-1, LAGS), table.T, precision=lax.Precision.HIGHEST).astype(jnp.bfloat16)
        response = lax.optimization_barrier(response).astype(jnp.float32).reshape(NBLK, STA, STA, 2 * FREQ)
        resp_re = response[..., :FREQ]
        resp_im = response[..., FREQ:]
        own_re = einsum_high('bijf,bjtf->bitf', resp_re, second[0]) - einsum_high('bijf,bjtf->bitf', resp_im, second[1])
        own_im = einsum_high('bijf,bjtf->bitf', resp_re, second[1]) + einsum_high('bijf,bjtf->bitf', resp_im, second[0])
        part_re = einsum_high('bijf,bitf->bjtf', resp_re, first[0]) + einsum_high('bijf,bitf->bjtf', resp_im, first[1])
        part_im = einsum_high('bijf,bitf->bjtf', resp_re, first[1]) - einsum_high('bijf,bitf->bjtf', resp_im, first[0])
        own_side = jnp.stack([own_re, own_im])
        partner_side = jnp.stack([part_re, part_im])
        summed = summed + own_side + jnp.roll(partner_side, offset, axis=1)
        return (summed, None)
    start_sum = jnp.zeros((2, NBLK, STA, WIN, FREQ), jnp.float32)
    summed, _ = lax.scan(one_offset, start_sum, jnp.arange(OFFSETS, dtype=jnp.int32))
    scaled = summed * (1.0 / math.sqrt(NSTA))
    block_rows = jnp.arange(NBLK, dtype=jnp.int32)[:, None]
    result = jnp.zeros_like(scaled).at[:, block_rows, station_slot.astype(jnp.int32)].set(scaled)
    return result.reshape(2, NSTA, WIN, FREQ)
```

```python
import math

import jax
import jax.numpy as jnp
import numpy as np
from jax import lax
from jax.experimental import pallas as pl
from jax.experimental.pallas import tpu as pltpu
from jax.sharding import PartitionSpec as P

MESH = pl.DeviceIdType.MESH
F32 = jnp.float32
BF16 = jnp.bfloat16


def angle_parts():
    lag = np.arange(1024, dtype=np.int64) - 512
    coarse = (np.arange(64, dtype=np.int64)[:, None] * 16 * lag[None]) % 2048
    fine = (np.arange(16, dtype=np.int64)[:, None] * lag[None]) % 2048
    scale = 1.0 / math.sqrt(8192.0)
    coarse = coarse * (math.pi / 1024)
    fine = fine * (math.pi / 1024)
    top = np.concatenate([np.cos(coarse), -np.sin(coarse)]) * scale
    low = np.concatenate([np.cos(fine), -np.sin(fine)])
    return top.astype(np.float32), low.astype(np.float32)


def place():
    blk = lax.axis_index("blk")
    lay = lax.axis_index("lay")
    x = lax.rem(lay, 4)
    y = lax.div(blk, 16)
    z = lax.div(lay, 4) * 8 + lax.div(lax.rem(blk, 16), 2)
    c = lax.rem(blk, 2)
    return blk, lay, x, y, z, c


def kernel(
    starts, ends, slots, spec_hbm, model_hbm, top_hbm, low_hbm, out,
    spec, model, top, low, raw, own_rows, ordered, partner, cross, left, table,
    model_rows, misfit, resp, own, part, outbox, inbox,
    load_sem, go_sem, come_sem, send_sem, recv_sem,
):
    blk, lay, x, y, z, c = place()
    loads = [
        pltpu.make_async_copy(spec_hbm, spec, load_sem.at[0]),
        pltpu.make_async_copy(top_hbm, top, load_sem.at[1]),
        pltpu.make_async_copy(low_hbm, low, load_sem.at[2]),
        pltpu.make_async_copy(model_hbm, model, load_sem.at[3]),
    ]
    for load in loads:
        load.start()
    loads[0].wait()
    for n in range(8):
        value = spec[n // 4, n % 4].astype(F32)
        for k in range(8):
            raw[pl.ds(n * 32 + k, 4, stride=8), :] = value[:, k * 128 : (k + 1) * 128]
    slot_of = [jnp.full((8, 128), slots[0, r], jnp.int32) for r in range(4)]
    chosen = [[slot_of[r] == q for q in range(4)] for r in range(4)]
    for n in range(8):
        for w in range(4):
            value = jnp.zeros((8, 128), F32)
            for q in range(4):
                at = ((n // 4) * 4 + q) * 32 + w * 8
                value = jnp.where(chosen[n % 4][q], raw[at : at + 8, :], value)
            own_rows[n * 32 + w * 8 : n * 32 + w * 8 + 8, :] = value
        ordered[n * 32 : (n + 1) * 32, :] = own_rows[n * 32 : (n + 1) * 32, :].astype(BF16)

    def forward(s):
        c2 = lax.rem(c + s, 2)
        far = 2 * x + lax.div(c2 + s, 2)
        z2 = lax.rem(z - far + 8 * lax.div(far + 3, 8) + 16, 16)
        y2 = lax.rem(y - lax.div(2 * z2 + c2 + 4 * x + s, 16) + 4, 4)
        return pltpu.make_async_remote_copy(
            src_ref=ordered,
            dst_ref=partner.at[s],
            send_sem=go_sem.at[s],
            recv_sem=come_sem.at[s],
            device_id=(
                y2 * 16 + lax.rem(z2, 8) * 2 + c2,
                lax.div(z2, 8) * 4 + x,
            ),
            device_id_type=MESH,
        )

    home = lay == 0

    @pl.when(home)
    def _():
        pltpu.make_async_copy(ordered, partner.at[0], come_sem.at[0]).start()

    @pl.when(jnp.logical_not(home))
    def _():
        forward(0).start()

    for s in range(1, 4):
        forward(s).start()

    loads[1].wait()
    loads[2].wait()

    @pl.loop(0, 64)
    def _(n):
        for q in range(4):
            at = slice(q * 256, (q + 1) * 256)
            cos_top = top[pl.ds(n, 1), at]
            sin_top = top[pl.ds(64 + n, 1), at]
            cos_low = low[0:16, at]
            sin_low = low[16:32, at]
            rows = pl.multiple_of(n * 16, 16)
            table[pl.ds(rows, 16), at] = (cos_top * cos_low - sin_top * sin_low).astype(BF16)
            table[pl.ds(1024 + rows, 16), at] = (sin_top * cos_low + cos_top * sin_low).astype(BF16)

    loads[3].wait()
    for n in range(16):
        model_rows[n * 4 : (n + 1) * 4, :] = model[0, n // 4, n % 4].astype(F32)

    @pl.when(home)
    def _():
        pltpu.make_async_copy(ordered, partner.at[0], come_sem.at[0]).wait()

    @pl.when(jnp.logical_not(home))
    def _():
        forward(0).wait()

    for s in range(1, 4):
        forward(s).wait()

    @pl.loop(0, 4)
    def _(s):
        re = [None] * 16
        im = [None] * 16
        for half in range(2):
            second = [
                partner[s, pl.ds(n * 32 + half * 16, 16), :].astype(F32) for n in range(8)
            ]
            for low_w in range(2):
                w = half * 2 + low_w
                first = [own_rows[n * 32 + w * 8 : n * 32 + w * 8 + 8, :] for n in range(8)]
                for i in range(4):
                    for j in range(4):
                        v_re = second[j][low_w * 8 : low_w * 8 + 8]
                        v_im = second[4 + j][low_w * 8 : low_w * 8 + 8]
                        a = first[i] * v_re + first[4 + i] * v_im
                        b = first[4 + i] * v_re - first[i] * v_im
                        n = i * 4 + j
                        re[n] = a if re[n] is None else re[n] + a
                        im[n] = b if im[n] is None else im[n] + b
        for n in range(16):
            at = pl.multiple_of(s * 128 + n * 8, 8)
            cross[pl.ds(at, 8), :] = re[n]
            cross[pl.ds(512 + at, 8), :] = im[n]

    for h in range(2):
        for k in range(8):
            left[:, h * 1024 + k * 128 : h * 1024 + (k + 1) * 128] = cross[
                pl.ds(h * 512 + k, 64, stride=8), :
            ].astype(BF16)

    row = lax.broadcasted_iota(jnp.int32, (64, 1), 0)
    offset = lax.div(row, 16)
    start = jnp.zeros((64, 1), jnp.int32)
    end = jnp.zeros((64, 1), jnp.int32)
    for s in range(4):
        start = jnp.where(offset == s, starts[0, s], start)
        end = jnp.where(offset == s, ends[0, s], end)
    diagonal = (lax.rem(lax.div(row, 4), 4) == lax.rem(row, 4)) & (offset == 0) & (lay == 0)
    end = jnp.where(diagonal, 0, end)

    @pl.loop(0, 4)
    def _(q):
        at = pl.multiple_of(q * 256, 256)
        lagged = jnp.dot(left[...], table[:, pl.ds(at, 256)], preferred_element_type=F32)
        lag = at + lax.broadcasted_iota(jnp.int32, (64, 256), 1)
        keep = (lag >= start) & (lag < end)
        misfit[:, pl.ds(at, 256)] = jnp.where(
            keep, lagged - model_rows[:, pl.ds(at, 256)], 0.0
        ).astype(BF16)

    @pl.loop(0, 8)
    def _(q):
        at = pl.multiple_of(q * 256, 256)
        value = lax.dot_general(
            misfit[...],
            table[pl.ds(at, 256), :],
            (((1,), (1,)), ((), ())),
            preferred_element_type=F32,
        )
        value = value.astype(BF16).astype(F32)
        base = lax.div(q, 4) * 512 + lax.rem(q, 4) * 2
        for k in range(2):
            resp[pl.ds(base + k, 64, stride=8), :] = value[:, k * 128 : (k + 1) * 128]

    @pl.loop(0, 4)
    def _(w):
        w8 = pl.multiple_of(w * 8, 8)
        w16 = pl.multiple_of(lax.div(w, 2) * 16, 16)
        odd = lax.rem(w, 2) == 1
        first = [own_rows[pl.ds(n * 32 + w8, 8), :] for n in range(8)]
        total = [jnp.zeros((8, 128), F32)] * 8
        for s in range(4):
            for j in range(4):
                pair_re = partner[s, pl.ds(j * 32 + w16, 16), :].astype(F32)
                pair_im = partner[s, pl.ds((4 + j) * 32 + w16, 16), :].astype(F32)
                v_re = jnp.where(odd, pair_re[8:], pair_re[:8])
                v_im = jnp.where(odd, pair_im[8:], pair_im[:8])
                part_re = jnp.zeros((8, 128), F32)
                part_im = jnp.zeros((8, 128), F32)
                for i in range(4):
                    at = (s * 16 + i * 4 + j) * 8
                    a = resp[at : at + 8, :]
                    b = resp[512 + at : 512 + at + 8, :]
                    total[i] = total[i] + (a * v_re - b * v_im)
                    total[4 + i] = total[4 + i] + (a * v_im + b * v_re)
                    part_re = part_re + (a * first[i] + b * first[4 + i])
                    part_im = part_im + (a * first[4 + i] - b * first[i])
                part[s, pl.ds(j * 32 + w8, 8), :] = part_re
                part[s, pl.ds((4 + j) * 32 + w8, 8), :] = part_im
        for n in range(8):
            own[pl.ds(n * 32 + w8, 8), :] = total[n]

    for k in range(8):
        outbox[32 + k] = own[pl.ds(k, 32, stride=8), :].astype(BF16)
        for s in range(4):
            outbox[k * 4 + s] = part[s, pl.ds(k, 32, stride=8), :].astype(BF16)

    def sends(n):
        s = lax.rem(n, 4)
        is_own = n >= 32
        to_lay = jnp.where(is_own, n - 32, lax.div(n, 4))
        to_blk = jnp.where(is_own, blk, lax.rem(blk + 4 * lay + s, 64))
        slot = jnp.where(is_own, 32 + lay, 4 * lay + s)
        return to_blk, to_lay, slot

    @pl.loop(0, 40)
    def _(n):
        to_blk, to_lay, slot = sends(n)
        here = (to_blk == blk) & (to_lay == lay)

        @pl.when(here)
        def _():
            pltpu.make_async_copy(outbox.at[n], inbox.at[slot], recv_sem).start()

        @pl.when(jnp.logical_not(here))
        def _():
            pltpu.make_async_remote_copy(
                src_ref=outbox.at[n],
                dst_ref=inbox.at[slot],
                send_sem=send_sem,
                recv_sem=recv_sem,
                device_id=(to_blk, to_lay),
                device_id_type=MESH,
            ).start()

    pltpu.make_async_copy(inbox, inbox, recv_sem).wait()

    @pl.when(home)
    def _():
        pltpu.make_async_copy(outbox.at[0:38], outbox.at[0:38], send_sem).wait()

    @pl.when(jnp.logical_not(home))
    def _():
        pltpu.make_async_copy(outbox.at[0:39], outbox.at[0:39], send_sem).wait()

    result = inbox[0].astype(F32)
    for n in range(1, 40):
        result = result + inbox[n].astype(F32)
    result = result * (1.0 / 16.0)
    raw[0:32, :] = result
    for p in range(2):
        for q in range(4):
            value = jnp.zeros((4, 128), F32)
            for r in range(4):
                at = p * 16 + r * 4
                value = jnp.where(chosen[r][q][:4], raw[at : at + 4, :], value)
            out[p, q] = value


def local(spectra, model_corr, window_start, window_end, station_slot):
    top, low = angle_parts()
    smem = pl.BlockSpec(memory_space=pltpu.SMEM)
    hbm = pl.BlockSpec(memory_space=pl.ANY)
    return pl.pallas_call(
        kernel,
        out_shape=jax.ShapeDtypeStruct((2, 4, 4, 128), F32),
        in_specs=[smem] * 3 + [hbm] * 4,
        out_specs=pl.BlockSpec(memory_space=pltpu.VMEM),
        scratch_shapes=[
            pltpu.VMEM((2, 4, 4, 1024), BF16),
            pltpu.VMEM((1, 4, 4, 4, 1024), BF16),
            pltpu.VMEM((128, 1024), F32),
            pltpu.VMEM((32, 1024), F32),
            pltpu.VMEM((256, 128), F32),
            pltpu.VMEM((256, 128), F32),
            pltpu.VMEM((256, 128), BF16),
            pltpu.VMEM((4, 256, 128), BF16),
            pltpu.VMEM((1024, 128), F32),
            pltpu.VMEM((64, 2048), BF16),
            pltpu.VMEM((2048, 1024), BF16),
            pltpu.VMEM((64, 1024), F32),
            pltpu.VMEM((64, 1024), BF16),
            pltpu.VMEM((1024, 128), F32),
            pltpu.VMEM((256, 128), F32),
            pltpu.VMEM((4, 256, 128), F32),
            pltpu.VMEM((40, 32, 128), BF16),
            pltpu.VMEM((40, 32, 128), BF16),
            pltpu.SemaphoreType.DMA((4,)),
            pltpu.SemaphoreType.DMA((4,)),
            pltpu.SemaphoreType.DMA((4,)),
            pltpu.SemaphoreType.DMA,
            pltpu.SemaphoreType.DMA,
        ],
        compiler_params=pltpu.CompilerParams(has_side_effects=True),
        name="adjoint",
    )(
        window_start, window_end, station_slot, spectra, model_corr,
        jnp.asarray(top), jnp.asarray(low),
    )


def solution(mesh):
    in_specs = (
        P(None, "blk", None, None),
        P("blk", "lay", None, None, None),
        P("blk", "lay"),
        P("blk", "lay"),
        P("blk", None),
    )
    out_specs = P(None, "blk", None, "lay")
    return jax.shard_map(local, mesh=mesh, in_specs=in_specs, out_specs=out_specs, check_vma=False)
```

```python
import math

import jax
import jax.numpy as jnp
import numpy as np
from jax import lax
from jax.experimental import pallas as pl
from jax.experimental.pallas import tpu as pltpu
from jax.sharding import PartitionSpec as P

MESH = pl.DeviceIdType.MESH
F32 = jnp.float32
BF16 = jnp.bfloat16

SOURCE = [[3, 1, 0, 0, 0], [2, 0, 1, 1, 1], [3, 2, 2, 2, 1], [3, 3, 0, 3, 2]]
AHEAD = [[0, 0, 1, 1, 2], [2, 2, 3, 3, -4], [4, 4, -3, -3, -2], [-2, -2, -1, -1, 0]]
SENT = [
    [[(x, q) for x in range(4) for q in range(core, 5, 2) if SOURCE[x][q] == source] for core in range(2)]
    for source in range(4)
]


def angle_parts():
    lag = np.arange(1024, dtype=np.int64) - 512
    coarse = (np.arange(64, dtype=np.int64)[:, None] * 16 * lag[None]) % 2048
    fine = (np.arange(16, dtype=np.int64)[:, None] * lag[None]) % 2048
    scale = 1.0 / math.sqrt(8192.0)
    coarse = coarse * (math.pi / 1024)
    fine = fine * (math.pi / 1024)
    top = np.concatenate([np.cos(coarse), -np.sin(coarse)]) * scale
    low = np.concatenate([np.cos(fine), -np.sin(fine)])
    return top.astype(np.float32), low.astype(np.float32)


def choose(index, values):
    result = jnp.int32(values[0])
    for n in range(1, len(values)):
        result = jnp.where(index == n, jnp.int32(values[n]), result)
    return result


def kernel(
    starts, ends, slots, spec_hbm, model_hbm, top_hbm, low_hbm, out,
    spec, model, top, low, raw, halves, ordered, peer_half, first, partner, cross, left, left_out,
    table, model_rows, lagged, misfit, resp, resp_out, resp_rows, own, part, outbox, inbox, merged, last,
    load_sem, peer_send, peer_recv, go_sem, come_sem, x_send, x_recv, z_send, z_recv,
):
    blk = lax.axis_index("blk")
    lay = lax.axis_index("lay")
    x = lax.rem(lay, 4)
    y = lax.div(blk, 16)
    zl = lax.div(lax.rem(blk, 16), 2)
    zh = lax.div(lay, 4)
    z = zh * 8 + zl
    c = lax.rem(blk, 2)
    other = 1 - c

    def device(x1, y1, z1, c1):
        return lax.rem(y1 + 8, 4) * 16 + lax.rem(z1, 8) * 2 + c1, lax.div(z1, 8) * 4 + x1

    peer = device(x, y, z, other)

    def receiver(n, core):
        to_x = jnp.where(
            c == 0,
            choose(x, [SENT[s][0][n][0] for s in range(4)]),
            choose(x, [SENT[s][1][min(n, 1)][0] for s in range(4)]),
        )
        q = jnp.where(
            c == 0,
            choose(x, [SENT[s][0][n][1] for s in range(4)]),
            choose(x, [SENT[s][1][min(n, 1)][1] for s in range(4)]),
        )
        ahead = jnp.where(
            c == 0,
            choose(x, [AHEAD[a][b] for a, b in (SENT[s][0][n] for s in range(4))]),
            choose(x, [AHEAD[a][b] for a, b in (SENT[s][1][min(n, 1)] for s in range(4))]),
        )
        to_z = lax.rem(z - ahead + 16, 16)
        to_y = y - lax.div(to_z + 2 * to_x + lax.div(q, 2), 8)
        return device(to_x, to_y, to_z, core), q

    def sender(q):
        from_z = lax.rem(z + choose(x, [AHEAD[s][q] for s in range(4)]) + 16, 16)
        from_y = y + lax.div(z + 2 * x + q // 2, 8)
        return device(choose(x, [SOURCE[s][q] for s in range(4)]), from_y, from_z, q % 2)

    def target(m):
        to_blk = 16 * y + 2 * zl + m - 17 if m >= 17 else lax.rem(16 * y + 2 * z + m, 64)
        slot = 16 + zh if m >= 17 else (m // 2) * 2 + zh + (2 if m == 16 else 0)
        return (to_blk, c * 4 + x), slot

    def elsewhere(to):
        return (to[0] != blk) | (to[1] != lay)

    barrier = pltpu.get_barrier_semaphore()

    def greet(to):
        pl.semaphore_signal(barrier, inc=1, device_id=to, device_id_type=MESH)

    for q in range(5):
        greet(sender(q))
    greet(peer)
    for t in range(1, 4):
        greet((blk, zh * 4 + lax.rem(x + t, 4)))
    for half in range(2):
        to = (16 * y + 2 * zl + zh, half * 4 + x)

        @pl.when(elsewhere(to))
        def _():
            greet(to)

        @pl.loop(0, 9 - c)
        def _(j):
            from_zl = lax.rem(zl - j + 8, 8)
            from_y = y - half + lax.div(zl - j + 8, 8) - 1
            to = device(x, from_y, half * 8 + from_zl, zh)

            @pl.when(elsewhere(to))
            def _():
                greet(to)

    loads = [
        pltpu.make_async_copy(spec_hbm, spec, load_sem.at[0]),
        pltpu.make_async_copy(top_hbm, top, load_sem.at[1]),
        pltpu.make_async_copy(low_hbm, low, load_sem.at[2]),
        pltpu.make_async_copy(model_hbm, model, load_sem.at[3]),
    ]
    for load in loads:
        load.start()
    with jax.named_scope("p01order"):
        loads[0].wait()
        for n in range(8):
            value = spec[n // 4, n % 4].astype(F32)
            for k in range(8):
                raw[pl.ds(n * 32 + k, 4, stride=8), :] = value[:, k * 128 : (k + 1) * 128]
        slot_of = [jnp.full((8, 128), slots[0, r], jnp.int32) for r in range(4)]
        chosen = [[slot_of[r] == q for q in range(4)] for r in range(4)]
        for p in range(2):
            for r in range(4):
                for w in range(4):
                    value = jnp.zeros((8, 128), F32)
                    for q in range(4):
                        at = (p * 4 + q) * 32 + w * 8
                        value = jnp.where(chosen[r][q], raw[at : at + 8, :], value)
                    at = ((p * 4 + w) * 4 + r) * 4
                    halves[0, at : at + 4, :] = value[:4]
                    halves[1, at : at + 4, :] = value[4:]
        for h in range(2):
            ordered[h] = halves[h].astype(BF16)

    with jax.named_scope("p02barrier"):
        mine = jnp.where(c == zh, 1, 0) + jnp.where((c == 0) & (zh == 0), 1, 0)
        pl.semaphore_wait(barrier, 23 + 6 - 2 * c - mine)

    peer_copy = pltpu.make_async_remote_copy(
        src_ref=ordered.at[other],
        dst_ref=peer_half,
        send_sem=peer_send.at[0],
        recv_sem=peer_recv.at[0],
        device_id=peer,
        device_id_type=MESH,
    )

    def forward(n, core):
        to, q = receiver(n, core)
        return pltpu.make_async_remote_copy(
            src_ref=ordered.at[core],
            dst_ref=partner.at[q],
            send_sem=go_sem.at[2 * n + core],
            recv_sem=come_sem.at[q],
            device_id=to,
            device_id_type=MESH,
        )

    with jax.named_scope("p03fwd"):
        for n in range(2):
            for core in range(2):
                forward(n, core).start()

        @pl.when(c == 0)
        def _():
            for core in range(2):
                forward(2, core).start()

        peer_copy.start()

    with jax.named_scope("p04table"):
        loads[1].wait()
        loads[2].wait()

        @pl.loop(0, 64)
        def _(n):
            h = lax.div(n, 32)
            at_row = pl.multiple_of(lax.rem(n, 32) * 16, 16)
            for q in range(4):
                at = slice(q * 256, (q + 1) * 256)
                cos_top = top[pl.ds(n, 1), at]
                sin_top = top[pl.ds(64 + n, 1), at]
                cos_low = low[0:16, at]
                sin_low = low[16:32, at]
                table[h, pl.ds(at_row, 16), at] = (cos_top * cos_low - sin_top * sin_low).astype(BF16)
                table[h, pl.ds(512 + at_row, 16), at] = (sin_top * cos_low + cos_top * sin_low).astype(BF16)

        loads[3].wait()
        for n in range(16):
            model_rows[n * 4 : (n + 1) * 4, :] = model[0, n // 4, n % 4].astype(F32)

        peer_copy.wait()
        for t in range(2):
            source = jnp.where(t == c, halves[c], peer_half[...].astype(F32))
            raw[0:128, :] = source
            for n in range(32):
                value = raw[n * 4 : n * 4 + 4, :]
                first[t, n * 8 : n * 8 + 4, :] = value
                first[t, n * 8 + 4 : n * 8 + 8, :] = value

    with jax.named_scope("p05fwdwait"):
        for q in range(5):
            pltpu.make_async_copy(partner.at[q], partner.at[q], come_sem.at[q]).wait()

    def cross_of(t):
        @pl.loop(0, 4)
        def _(s):
            re = [None] * 8
            im = [None] * 8
            for w in range(4):
                u = [
                    first[t, ((p * 4 + w) * 4 + i) * 8 : ((p * 4 + w) * 4 + i) * 8 + 8, :]
                    for p in range(2)
                    for i in range(4)
                ]
                v_re = partner[t + s, w * 16 : w * 16 + 16, :].astype(F32)
                v_im = partner[t + s, 64 + w * 16 : 64 + w * 16 + 16, :].astype(F32)
                for i in range(4):
                    for jp in range(2):
                        a_re = v_re[jp * 8 : jp * 8 + 8]
                        a_im = v_im[jp * 8 : jp * 8 + 8]
                        a = u[i] * a_re + u[4 + i] * a_im
                        b = u[4 + i] * a_re - u[i] * a_im
                        n = i * 2 + jp
                        re[n] = a if w == 0 else re[n] + a
                        im[n] = b if w == 0 else im[n] + b
            for n in range(8):
                at = pl.multiple_of(s * 64 + n * 8, 8)
                cross[pl.ds(at, 8), :] = re[n]
                cross[pl.ds(256 + at, 8), :] = im[n]

    def gather(into):
        for h in range(2):
            for k in range(4):
                into[:, h * 512 + k * 128 : h * 512 + (k + 1) * 128] = cross[
                    pl.ds(h * 256 + k, 64, stride=4), :
                ].astype(BF16)

    left_copy = pltpu.make_async_remote_copy(
        src_ref=left_out,
        dst_ref=left.at[1],
        send_sem=peer_send.at[1],
        recv_sem=peer_recv.at[1],
        device_id=peer,
        device_id_type=MESH,
    )
    with jax.named_scope("p06cross"):
        cross_of(other)
        gather(left_out)
        left_copy.start()
        cross_of(c)
        gather(left.at[0])

    with jax.named_scope("p07lag"):
        @pl.loop(0, 4)
        def _(q):
            at = pl.multiple_of(q * 256, 256)
            lagged[:, pl.ds(at, 256)] = jnp.dot(
                left[0], table[c, :, pl.ds(at, 256)], preferred_element_type=F32
            )

        row = lax.broadcasted_iota(jnp.int32, (64, 1), 0)
        offset = lax.div(row, 16)
        start = jnp.zeros((64, 1), jnp.int32)
        end = jnp.zeros((64, 1), jnp.int32)
        for s in range(4):
            start = jnp.where(offset == s, starts[0, s], start)
            end = jnp.where(offset == s, ends[0, s], end)
        diagonal = (lax.rem(lax.div(row, 4), 4) == lax.rem(row, 4)) & (offset == 0) & (lay == 0)
        end = jnp.where(diagonal, 0, end)
        left_copy.wait()

        @pl.loop(0, 4)
        def _(q):
            at = pl.multiple_of(q * 256, 256)
            value = lagged[:, pl.ds(at, 256)] + jnp.dot(
                left[1], table[other, :, pl.ds(at, 256)], preferred_element_type=F32
            )
            lag = at + lax.broadcasted_iota(jnp.int32, (64, 256), 1)
            keep = (lag >= start) & (lag < end)
            misfit[:, pl.ds(at, 256)] = jnp.where(
                keep, value - model_rows[:, pl.ds(at, 256)], 0.0
            ).astype(BF16)

    resp_copy = pltpu.make_async_remote_copy(
        src_ref=resp_out,
        dst_ref=resp.at[1],
        send_sem=peer_send.at[2],
        recv_sem=peer_recv.at[2],
        device_id=peer,
        device_id_type=MESH,
    )

    def respond(h, into):
        @pl.loop(0, 4)
        def _(q):
            at = pl.multiple_of(q * 256, 256)
            into[:, pl.ds(at, 256)] = lax.dot_general(
                misfit[...],
                table[h, pl.ds(at, 256), :],
                (((1,), (1,)), ((), ())),
                preferred_element_type=F32,
            ).astype(BF16)

    def spread(n, t):
        for p in range(2):
            for k in range(4):
                resp_rows[t, pl.ds(p * 256 + k, 64, stride=4), :] = resp[
                    n, :, p * 512 + k * 128 : p * 512 + (k + 1) * 128
                ].astype(F32)

    with jax.named_scope("p08resp"):
        respond(other, resp_out)
        resp_copy.start()
        respond(c, resp.at[0])
        spread(0, c)
        resp_copy.wait()
        spread(1, other)

    with jax.named_scope("p09terms"):

        @pl.loop(0, 4)
        def _(w):
            at_u = [pl.multiple_of(((p * 4 + w) * 4) * 8, 8) for p in range(2)]
            at_v = [pl.multiple_of((p * 4 + w) * 16, 16) for p in range(2)]
            u = [
                [first[t, pl.ds(at_u[p] + i * 8, 8), :] for p in range(2) for i in range(4)]
                for t in range(2)
            ]
            total = [[jnp.zeros((8, 128), F32)] * 8 for t in range(2)]
            for q in range(5):
                v = [partner[q, pl.ds(at_v[p], 16), :].astype(F32) for p in range(2)]
                for jp in range(2):
                    v_re = v[0][jp * 8 : jp * 8 + 8]
                    v_im = v[1][jp * 8 : jp * 8 + 8]
                    part_re = jnp.zeros((8, 128), F32)
                    part_im = jnp.zeros((8, 128), F32)
                    for t in range(2):
                        s = q - t
                        if not 0 <= s < 4:
                            continue
                        for i in range(4):
                            at = ((s * 4 + i) * 2 + jp) * 8
                            a = resp_rows[t, at : at + 8, :]
                            b = resp_rows[t, 256 + at : 256 + at + 8, :]
                            total[t][i] = total[t][i] + (a * v_re - b * v_im)
                            total[t][4 + i] = total[t][4 + i] + (a * v_im + b * v_re)
                            part_re = part_re + (a * u[t][i] + b * u[t][4 + i])
                            part_im = part_im + (a * u[t][4 + i] - b * u[t][i])
                    part[q, pl.ds(at_v[0] + jp * 8, 8), :] = part_re
                    part[q, pl.ds(at_v[1] + jp * 8, 8), :] = part_im
            for t in range(2):
                for p in range(2):
                    for i in range(4):
                        own[t, pl.ds(((p * 4 + i) * 4 + w) * 8, 8), :] = total[t][p * 4 + i]

    with jax.named_scope("p10pack"):
        for k in range(4):
            for t in range(2):
                outbox[k, 5 + t] = (
                    own[t, pl.ds(k, 32, stride=8), :] + own[t, pl.ds(4 + k, 32, stride=8), :]
                ).astype(BF16)
            for q in range(5):
                outbox[k, q] = part[q, pl.ds(k, 32, stride=4), :].astype(BF16)

    def across(t):
        to = lax.rem(x + t, 4)
        return pltpu.make_async_remote_copy(
            src_ref=outbox.at[to],
            dst_ref=inbox.at[x],
            send_sem=x_send.at[t - 1],
            recv_sem=x_recv.at[x],
            device_id=(blk, zh * 4 + to),
            device_id_type=MESH,
        )

    def deliver(source, m):
        to, slot = target(m)

        def start():
            pltpu.make_async_remote_copy(
                src_ref=source,
                dst_ref=last.at[slot],
                send_sem=z_send,
                recv_sem=z_recv,
                device_id=to,
                device_id_type=MESH,
            ).start()

        if m in (0, 17, 18):
            away = elsewhere(to)
            pl.when(away)(start)

            @pl.when(jnp.logical_not(away))
            def _():
                pltpu.make_async_copy(source, last.at[slot], z_recv).start()
        else:
            start()

    with jax.named_scope("p11x"):
        for t in (2, 1, 3):
            across(t).start()
        keep_copy = pltpu.make_async_copy(outbox.at[x], inbox.at[x], x_recv.at[x])
        keep_copy.start()
        for n in range(4):
            pltpu.make_async_copy(inbox.at[n], inbox.at[n], x_recv.at[n]).wait()

    with jax.named_scope("p12merge"):
        for n in range(4):
            for r in range(1, 4):
                deliver(inbox.at[n, r], 4 * n + r)
        deliver(inbox.at[0, 0], 0)
        deliver(inbox.at[3, 4], 16)
        for t in range(2):
            value = inbox[0, 5 + t].astype(F32)
            for n in range(1, 4):
                value = value + inbox[n, 5 + t].astype(F32)
            merged[3 + t] = value.astype(BF16)
        for n in range(1, 4):
            merged[n - 1] = (inbox[n, 0].astype(F32) + inbox[n - 1, 4].astype(F32)).astype(BF16)
        for n in range(1, 4):
            deliver(merged.at[n - 1], 4 * n)
        for t in range(2):
            deliver(merged.at[3 + t], 17 + t)

    with jax.named_scope("p13wait"):

        @pl.when(c == 0)
        def _():
            pltpu.make_async_copy(last, last, z_recv).wait()

        @pl.when(c == 1)
        def _():
            pltpu.make_async_copy(last.at[0:18], last.at[0:18], z_recv).wait()

    with jax.named_scope("p14sum"):
        total = last[0].astype(F32)
        for n in range(1, 16):
            total = total + last[n].astype(F32)
        scale = 1.0 / 16.0
        raw[32:64, :] = (last[16].astype(F32) + last[17].astype(F32)) * scale

        @pl.when(c == 0)
        def _():
            raw[0:32, :] = (total + last[18].astype(F32) + last[19].astype(F32)) * scale

        @pl.when(c == 1)
        def _():
            raw[0:32, :] = total * scale

        for p in range(2):
            row_of = [
                raw[pl.ds(p * 16 + r, 4, stride=4), :]
                + raw[32 + p * 16 + r * 4 : 32 + p * 16 + r * 4 + 4, :]
                for r in range(4)
            ]
            for q in range(4):
                value = jnp.zeros((4, 128), F32)
                for r in range(4):
                    value = jnp.where(chosen[r][q][:4], row_of[r], value)
                out[p, q] = value

        for n in range(2):
            for core in range(2):
                forward(n, core).wait_send()

        @pl.when(c == 0)
        def _():
            for core in range(2):
                forward(2, core).wait_send()

        for t in range(1, 4):
            across(t).wait_send()
        for n in range(3):

            @pl.when(mine == n)
            def _():
                gone = last.at[0 : 19 - n]
                pltpu.make_async_copy(gone, gone, z_send).wait()


def local(spectra, model_corr, window_start, window_end, station_slot):
    top, low = angle_parts()
    smem = pl.BlockSpec(memory_space=pltpu.SMEM)
    hbm = pl.BlockSpec(memory_space=pl.ANY)
    dma = pltpu.SemaphoreType.DMA
    return pl.pallas_call(
        kernel,
        out_shape=jax.ShapeDtypeStruct((2, 4, 4, 128), F32),
        in_specs=[smem] * 3 + [hbm] * 4,
        out_specs=pl.BlockSpec(memory_space=pltpu.VMEM),
        scratch_shapes=[
            pltpu.VMEM((2, 4, 4, 1024), BF16),
            pltpu.VMEM((1, 4, 4, 4, 1024), BF16),
            pltpu.VMEM((128, 1024), F32),
            pltpu.VMEM((32, 1024), F32),
            pltpu.VMEM((256, 128), F32),
            pltpu.VMEM((2, 128, 128), F32),
            pltpu.VMEM((2, 128, 128), BF16),
            pltpu.VMEM((128, 128), BF16),
            pltpu.VMEM((2, 256, 128), F32),
            pltpu.VMEM((5, 128, 128), BF16),
            pltpu.VMEM((512, 128), F32),
            pltpu.VMEM((2, 64, 1024), BF16),
            pltpu.VMEM((64, 1024), BF16),
            pltpu.VMEM((2, 1024, 1024), BF16),
            pltpu.VMEM((64, 1024), F32),
            pltpu.VMEM((64, 1024), F32),
            pltpu.VMEM((64, 1024), BF16),
            pltpu.VMEM((2, 64, 1024), BF16),
            pltpu.VMEM((64, 1024), BF16),
            pltpu.VMEM((2, 512, 128), F32),
            pltpu.VMEM((2, 256, 128), F32),
            pltpu.VMEM((5, 128, 128), F32),
            pltpu.VMEM((4, 7, 32, 128), BF16),
            pltpu.VMEM((4, 7, 32, 128), BF16),
            pltpu.VMEM((5, 32, 128), BF16),
            pltpu.VMEM((20, 32, 128), BF16),
            dma((4,)), dma((3,)), dma((3,)), dma((6,)), dma((5,)), dma((3,)), dma((4,)), dma, dma,
        ],
        compiler_params=pltpu.CompilerParams(has_side_effects=True, collective_id=0),
        name="adjoint",
    )(
        window_start, window_end, station_slot, spectra, model_corr,
        jnp.asarray(top), jnp.asarray(low),
    )


def solution(mesh):
    in_specs = (
        P(None, "blk", None, None),
        P("blk", "lay", None, None, None),
        P("blk", "lay"),
        P("blk", "lay"),
        P("blk", None),
    )
    out_specs = P(None, "blk", None, "lay")
    return jax.shard_map(local, mesh=mesh, in_specs=in_specs, out_specs=out_specs, check_vma=False)
```

```python
import math

import jax
import jax.numpy as jnp
import numpy as np
from jax import lax
from jax.experimental import pallas as pl
from jax.experimental.pallas import tpu as pltpu
from jax.sharding import PartitionSpec as P

MESH = pl.DeviceIdType.MESH
F32 = jnp.float32
BF16 = jnp.bfloat16

SOURCE = [[3, 1, 0, 0, 0], [2, 0, 1, 1, 1], [3, 2, 2, 2, 1], [3, 3, 0, 3, 2]]
AHEAD = [[0, 0, 1, 1, 2], [2, 2, 3, 3, -4], [4, 4, -3, -3, -2], [-2, -2, -1, -1, 0]]
SENT = [
    [[(x, q) for x in range(4) for q in range(core, 5, 2) if SOURCE[x][q] == source] for core in range(2)]
    for source in range(4)
]


def angle_parts():
    lag = np.arange(1024, dtype=np.int64) - 512
    coarse = (np.arange(64, dtype=np.int64)[:, None] * 16 * lag[None]) % 2048
    fine = (np.arange(16, dtype=np.int64)[:, None] * lag[None]) % 2048
    scale = 1.0 / math.sqrt(8192.0)
    coarse = coarse * (math.pi / 1024)
    fine = fine * (math.pi / 1024)
    top = np.concatenate([np.cos(coarse), -np.sin(coarse)]) * scale
    low = np.concatenate([np.cos(fine), -np.sin(fine)])
    freq = np.arange(1024, dtype=np.int64)
    coarse = ((np.arange(64, dtype=np.int64)[:, None] * 16 - 512) * freq[None]) % 2048
    fine = (np.arange(16, dtype=np.int64)[:, None] * freq[None]) % 2048
    coarse = coarse * (math.pi / 1024)
    fine = fine * (math.pi / 1024)
    top2 = np.concatenate([np.cos(coarse), -np.sin(coarse)]) * scale
    low2 = np.concatenate([np.cos(fine), -np.sin(fine)])
    both = np.stack([np.concatenate([top, low]), np.concatenate([top2, low2])])
    return both.astype(np.float32)


def choose(index, values):
    result = jnp.int32(values[0])
    for n in range(1, len(values)):
        result = jnp.where(index == n, jnp.int32(values[n]), result)
    return result


def kernel(
    starts_hbm, ends_hbm, slots_hbm, spec_hbm, model_hbm, angles_hbm, out,
    starts, ends, slots, spec, model, angles, raw, halves, ordered, peer_half, first, partner, cross, left, left_out,
    table, turned, model_rows, lagged, misfit, resp, resp_out, resp_rows, own, part, outbox, inbox, merged, last,
    load_sem, ring_sem, peer_send, peer_recv, go_sem, come_sem, x_send, x_recv, z_send, z_recv,
):
    blk = lax.axis_index("blk")
    lay = lax.axis_index("lay")
    x = lax.rem(lay, 4)
    y = lax.div(blk, 16)
    zl = lax.div(lax.rem(blk, 16), 2)
    zh = lax.div(lay, 4)
    z = zh * 8 + zl
    c = lax.rem(blk, 2)
    other = 1 - c

    def device(x1, y1, z1, c1):
        return lax.rem(y1 + 8, 4) * 16 + lax.rem(z1, 8) * 2 + c1, lax.div(z1, 8) * 4 + x1

    peer = device(x, y, z, other)

    def receiver(n, core):
        to_x = jnp.where(
            c == 0,
            choose(x, [SENT[s][0][n][0] for s in range(4)]),
            choose(x, [SENT[s][1][min(n, 1)][0] for s in range(4)]),
        )
        q = jnp.where(
            c == 0,
            choose(x, [SENT[s][0][n][1] for s in range(4)]),
            choose(x, [SENT[s][1][min(n, 1)][1] for s in range(4)]),
        )
        ahead = jnp.where(
            c == 0,
            choose(x, [AHEAD[a][b] for a, b in (SENT[s][0][n] for s in range(4))]),
            choose(x, [AHEAD[a][b] for a, b in (SENT[s][1][min(n, 1)] for s in range(4))]),
        )
        to_z = lax.rem(z - ahead + 16, 16)
        to_y = y - lax.div(to_z + 2 * to_x + lax.div(q, 2), 8)
        return device(to_x, to_y, to_z, core), q

    def sender(q):
        from_z = lax.rem(z + choose(x, [AHEAD[s][q] for s in range(4)]) + 16, 16)
        from_y = y + lax.div(z + 2 * x + q // 2, 8)
        return device(choose(x, [SOURCE[s][q] for s in range(4)]), from_y, from_z, q % 2)

    mine = jnp.where(c == zh, 1, 0) + jnp.where((c == 0) & (zh == 0), 1, 0)

    def target(m):
        if isinstance(m, int) and m >= 17:
            return (16 * y + 2 * zl + m - 17, c * 4 + x), 16 + zh
        slot = lax.div(m, 2) * 2 + zh + (2 if isinstance(m, int) and m == 16 else 0)
        return (lax.rem(16 * y + 2 * z + m, 64), c * 4 + x), slot

    def elsewhere(to):
        return (to[0] != blk) | (to[1] != lay)

    loads = [
        pltpu.make_async_copy(spec_hbm, spec, load_sem.at[0]),
        pltpu.make_async_copy(slots_hbm, slots, load_sem.at[1]),
        pltpu.make_async_copy(angles_hbm, angles, load_sem.at[2]),
        pltpu.make_async_copy(model_hbm, model, load_sem.at[3]),
        pltpu.make_async_copy(starts_hbm, starts, load_sem.at[4]),
        pltpu.make_async_copy(ends_hbm, ends, load_sem.at[5]),
    ]
    for load in loads:
        load.start()

    barrier = pltpu.get_barrier_semaphore()

    def greet(to):
        pl.semaphore_signal(barrier, inc=1, device_id=to, device_id_type=MESH)

    for q in range(5):
        greet(sender(q))
    greet(peer)
    for t in range(1, 4):
        greet((blk, zh * 4 + lax.rem(x + t, 4)))
    near = [
        [device(x, y + d, z, c) for d in (-1, 1)],
        [device(x, y, lax.rem(z + d + 16, 16), c) for d in (-1, 1)],
        [device(x, y, lax.rem(z + d + 16, 16), c) for d in (-2, 2)],
        [device(x, y, lax.rem(z + d + 16, 16), c) for d in (-4, 4)],
        [device(x, y + d, z, c) for d in (-1, 1)],
    ]
    for pair in near[:2]:
        for to in pair:
            greet(to)

    def tell(n):
        for to in near[n]:
            pl.semaphore_signal(ring_sem.at[n], inc=1, device_id=to, device_id_type=MESH)

    def told(n):
        pl.semaphore_wait(ring_sem.at[n], 2)

    with jax.named_scope("p01order"):
        loads[0].wait()
        loads[1].wait()
        for n in range(8):
            value = spec[n // 4, n % 4].astype(F32)
            for k in range(8):
                raw[pl.ds(n * 32 + k, 4, stride=8), :] = value[:, k * 128 : (k + 1) * 128]
        slot_of = [jnp.full((8, 128), slots[0, r], jnp.int32) for r in range(4)]
        chosen = [[slot_of[r] == q for q in range(4)] for r in range(4)]
        for p in range(2):
            for r in range(4):
                for w in range(4):
                    value = jnp.zeros((8, 128), F32)
                    for q in range(4):
                        at = (p * 4 + q) * 32 + w * 8
                        value = jnp.where(chosen[r][q], raw[at : at + 8, :], value)
                    at = ((p * 4 + w) * 4 + r) * 4
                    halves[0, at : at + 4, :] = value[:4]
                    halves[1, at : at + 4, :] = value[4:]
        for h in range(2):
            ordered[h] = halves[h].astype(BF16)

    with jax.named_scope("p01table"):
        loads[2].wait()

        @pl.loop(0, 64)
        def _(n):
            h = lax.div(n, 32)
            at_row = pl.multiple_of(lax.rem(n, 32) * 16, 16)
            for q in range(4):
                at = slice(q * 256, (q + 1) * 256)
                cos_top = angles[0, pl.ds(n, 1), at]
                sin_top = angles[0, pl.ds(64 + n, 1), at]
                cos_low = angles[0, 128:144, at]
                sin_low = angles[0, 144:160, at]
                table[h, pl.ds(at_row, 16), at] = (cos_top * cos_low - sin_top * sin_low).astype(BF16)
                table[h, pl.ds(512 + at_row, 16), at] = (sin_top * cos_low + cos_top * sin_low).astype(BF16)

    with jax.named_scope("p02barrier"):
        pl.semaphore_wait(barrier, 8 + 6 - 2 * c)
        tell(0)

    peer_copy = pltpu.make_async_remote_copy(
        src_ref=ordered.at[other],
        dst_ref=peer_half,
        send_sem=peer_send.at[0],
        recv_sem=peer_recv.at[0],
        device_id=peer,
        device_id_type=MESH,
    )

    def forward(n, core):
        to, q = receiver(n, core)
        return pltpu.make_async_remote_copy(
            src_ref=ordered.at[core],
            dst_ref=partner.at[q],
            send_sem=go_sem.at[2 * n + core],
            recv_sem=come_sem.at[q],
            device_id=to,
            device_id_type=MESH,
        )

    with jax.named_scope("p03fwd"):
        for n in range(2):
            for core in range(2):
                forward(n, core).start()

        @pl.when(c == 0)
        def _():
            for core in range(2):
                forward(2, core).start()

        peer_copy.start()

    with jax.named_scope("p04table"):
        told(0)
        tell(1)

        @pl.loop(0, 64)
        def _(n):
            at_row = pl.multiple_of(n * 16, 16)
            for q in range(4):
                at = slice(q * 256, (q + 1) * 256)
                to = slice((q % 2) * 256, (q % 2) * 256 + 256)
                to_sin = slice(512 + (q % 2) * 256, 512 + (q % 2) * 256 + 256)
                cos_top = angles[1, pl.ds(n, 1), at]
                sin_top = angles[1, pl.ds(64 + n, 1), at]
                cos_low = angles[1, 128:144, at]
                sin_low = angles[1, 144:160, at]
                turned[q // 2, pl.ds(at_row, 16), to] = (cos_top * cos_low - sin_top * sin_low).astype(BF16)
                turned[q // 2, pl.ds(at_row, 16), to_sin] = (sin_top * cos_low + cos_top * sin_low).astype(BF16)

        told(1)
        tell(2)
        loads[3].wait()
        for n in range(16):
            model_rows[n * 4 : (n + 1) * 4, :] = model[0, n // 4, n % 4].astype(F32)

        peer_copy.wait()
        for t in range(2):
            source = jnp.where(t == c, halves[c], peer_half[...].astype(F32))
            raw[0:128, :] = source
            for n in range(32):
                value = raw[n * 4 : n * 4 + 4, :]
                first[t, n * 8 : n * 8 + 4, :] = value
                first[t, n * 8 + 4 : n * 8 + 8, :] = value

    with jax.named_scope("p05fwdwait"):
        for q in range(5):
            pltpu.make_async_copy(partner.at[q], partner.at[q], come_sem.at[q]).wait()
        told(2)
        tell(3)

    def cross_of(t):
        @pl.loop(0, 4)
        def _(s):
            re = [None] * 8
            im = [None] * 8
            for w in range(4):
                u = [
                    first[t, ((p * 4 + w) * 4 + i) * 8 : ((p * 4 + w) * 4 + i) * 8 + 8, :]
                    for p in range(2)
                    for i in range(4)
                ]
                v_re = partner[t + s, w * 16 : w * 16 + 16, :].astype(F32)
                v_im = partner[t + s, 64 + w * 16 : 64 + w * 16 + 16, :].astype(F32)
                for i in range(4):
                    for jp in range(2):
                        a_re = v_re[jp * 8 : jp * 8 + 8]
                        a_im = v_im[jp * 8 : jp * 8 + 8]
                        a = u[i] * a_re + u[4 + i] * a_im
                        b = u[4 + i] * a_re - u[i] * a_im
                        n = i * 2 + jp
                        re[n] = a if w == 0 else re[n] + a
                        im[n] = b if w == 0 else im[n] + b
            for n in range(8):
                at = pl.multiple_of(s * 64 + n * 8, 8)
                cross[pl.ds(at, 8), :] = re[n]
                cross[pl.ds(256 + at, 8), :] = im[n]

    def gather(into):
        for h in range(2):
            for k in range(4):
                into[:, h * 512 + k * 128 : h * 512 + (k + 1) * 128] = cross[
                    pl.ds(h * 256 + k, 64, stride=4), :
                ].astype(BF16)

    left_copy = pltpu.make_async_remote_copy(
        src_ref=left_out,
        dst_ref=left.at[1],
        send_sem=peer_send.at[1],
        recv_sem=peer_recv.at[1],
        device_id=peer,
        device_id_type=MESH,
    )
    with jax.named_scope("p06cross"):
        cross_of(other)
        gather(left_out)
        left_copy.start()
        cross_of(c)
        gather(left.at[0])

    with jax.named_scope("p07lag"):
        lagged[...] = jnp.dot(left[0], table[c], preferred_element_type=F32)

        loads[4].wait()
        loads[5].wait()
        row = lax.broadcasted_iota(jnp.int32, (64, 1), 0)
        offset = lax.div(row, 16)
        start = jnp.zeros((64, 1), jnp.int32)
        end = jnp.zeros((64, 1), jnp.int32)
        for s in range(4):
            start = jnp.where(offset == s, starts[0, s], start)
            end = jnp.where(offset == s, ends[0, s], end)
        diagonal = (lax.rem(lax.div(row, 4), 4) == lax.rem(row, 4)) & (offset == 0) & (lay == 0)
        end = jnp.where(diagonal, 0, end)
        left_copy.wait()
        value = lagged[...] + jnp.dot(left[1], table[other], preferred_element_type=F32)
        lag = lax.broadcasted_iota(jnp.int32, (64, 1024), 1)
        keep = (lag >= start) & (lag < end)
        misfit[...] = jnp.where(keep, value - model_rows[...], 0.0).astype(BF16)

    resp_copy = pltpu.make_async_remote_copy(
        src_ref=resp_out,
        dst_ref=resp.at[1],
        send_sem=peer_send.at[2],
        recv_sem=peer_recv.at[2],
        device_id=peer,
        device_id_type=MESH,
    )

    def respond(h, into):
        into[...] = jnp.dot(misfit[...], turned[h], preferred_element_type=F32).astype(BF16)

    def spread(n, t):
        for p in range(2):
            for k in range(4):
                resp_rows[t, pl.ds(p * 256 + k, 64, stride=4), :] = resp[
                    n, :, p * 512 + k * 128 : p * 512 + (k + 1) * 128
                ].astype(F32)

    def terms_of(t):
        @pl.loop(0, 4)
        def _(w):
            at_u = [pl.multiple_of(((p * 4 + w) * 4) * 8, 8) for p in range(2)]
            at_v = [pl.multiple_of((p * 4 + w) * 16, 16) for p in range(2)]
            u = [first[t, pl.ds(at_u[p] + i * 8, 8), :] for p in range(2) for i in range(4)]
            total = [jnp.zeros((8, 128), F32)] * 8
            for s in range(4):
                v = [partner[t + s, pl.ds(at_v[p], 16), :].astype(F32) for p in range(2)]
                for jp in range(2):
                    v_re = v[0][jp * 8 : jp * 8 + 8]
                    v_im = v[1][jp * 8 : jp * 8 + 8]
                    part_re = jnp.zeros((8, 128), F32)
                    part_im = jnp.zeros((8, 128), F32)
                    for i in range(4):
                        at = ((s * 4 + i) * 2 + jp) * 8
                        a = resp_rows[t, at : at + 8, :]
                        b = resp_rows[t, 256 + at : 256 + at + 8, :]
                        total[i] = total[i] + (a * v_re - b * v_im)
                        total[4 + i] = total[4 + i] + (a * v_im + b * v_re)
                        part_re = part_re + (a * u[i] + b * u[4 + i])
                        part_im = part_im + (a * u[4 + i] - b * u[i])
                    part[t, s, pl.ds(at_v[0] + jp * 8, 8), :] = part_re
                    part[t, s, pl.ds(at_v[1] + jp * 8, 8), :] = part_im
            for p in range(2):
                for i in range(4):
                    own[t, pl.ds(((p * 4 + i) * 4 + w) * 8, 8), :] = total[p * 4 + i]

    with jax.named_scope("p08resp"):

        @pl.when(c == 0)
        def _():
            respond(0, resp.at[0])
            respond(1, resp_out)
            resp_copy.start()

        @pl.when(c == 1)
        def _():
            respond(0, resp_out)
            resp_copy.start()
            respond(1, resp.at[0])

        spread(0, c)
        terms_of(c)
        resp_copy.wait()

    with jax.named_scope("p09terms"):
        spread(1, other)
        terms_of(other)

    with jax.named_scope("p10pack"):
        for k in range(4):
            for t in range(2):
                outbox[k, 5 + t] = (
                    own[t, pl.ds(k, 32, stride=8), :] + own[t, pl.ds(4 + k, 32, stride=8), :]
                ).astype(BF16)
            for q in range(5):
                value = [part[t, q - t, pl.ds(k, 32, stride=4), :] for t in range(2) if 0 <= q - t < 4]
                outbox[k, q] = (value[0] if len(value) == 1 else value[0] + value[1]).astype(BF16)

    def across(t):
        to = lax.rem(x + t, 4)
        return pltpu.make_async_remote_copy(
            src_ref=outbox.at[to],
            dst_ref=inbox.at[x],
            send_sem=x_send.at[t - 1],
            recv_sem=x_recv.at[x],
            device_id=(blk, zh * 4 + to),
            device_id_type=MESH,
        )

    def deliver(source, m):
        to, slot = target(m)

        def start():
            pltpu.make_async_remote_copy(
                src_ref=source,
                dst_ref=last.at[slot],
                send_sem=z_send,
                recv_sem=z_recv,
                device_id=to,
                device_id_type=MESH,
            ).start()

        if isinstance(m, int) and m in (0, 17, 18):
            away = elsewhere(to)
            pl.when(away)(start)

            @pl.when(jnp.logical_not(away))
            def _():
                pltpu.make_async_copy(source, last.at[slot], z_recv).start()
        else:
            start()

    with jax.named_scope("p11x"):
        for t in (2, 1, 3):
            across(t).start()
        keep_copy = pltpu.make_async_copy(outbox.at[x], inbox.at[x], x_recv.at[x])
        keep_copy.start()
        told(3)
        tell(4)
        told(4)
        for t in (0, 1, 3, 2):
            n = lax.rem(x + t, 4)
            pltpu.make_async_copy(inbox.at[n], inbox.at[n], x_recv.at[n]).wait()
            for r in range(1, 4):
                deliver(inbox.at[n, r], 4 * n + r)

    with jax.named_scope("p12merge"):
        deliver(inbox.at[0, 0], 0)
        deliver(inbox.at[3, 4], 16)
        for t in range(2):
            value = inbox[0, 5 + t].astype(F32)
            for n in range(1, 4):
                value = value + inbox[n, 5 + t].astype(F32)
            merged[3 + t] = value.astype(BF16)
        for n in range(1, 4):
            merged[n - 1] = (inbox[n, 0].astype(F32) + inbox[n - 1, 4].astype(F32)).astype(BF16)
        for n in range(1, 4):
            deliver(merged.at[n - 1], 4 * n)
        for t in range(2):
            deliver(merged.at[3 + t], 17 + t)

    with jax.named_scope("p13wait"):

        @pl.when(c == 0)
        def _():
            pltpu.make_async_copy(last, last, z_recv).wait()

        @pl.when(c == 1)
        def _():
            pltpu.make_async_copy(last.at[0:18], last.at[0:18], z_recv).wait()

    with jax.named_scope("p14sum"):
        total = last[0].astype(F32)
        for n in range(1, 16):
            total = total + last[n].astype(F32)
        scale = 1.0 / 16.0
        raw[32:64, :] = (last[16].astype(F32) + last[17].astype(F32)) * scale

        @pl.when(c == 0)
        def _():
            raw[0:32, :] = (total + last[18].astype(F32) + last[19].astype(F32)) * scale

        @pl.when(c == 1)
        def _():
            raw[0:32, :] = total * scale

        for p in range(2):
            row_of = [
                raw[pl.ds(p * 16 + r, 4, stride=4), :]
                + raw[32 + p * 16 + r * 4 : 32 + p * 16 + r * 4 + 4, :]
                for r in range(4)
            ]
            for q in range(4):
                value = jnp.zeros((4, 128), F32)
                for r in range(4):
                    value = jnp.where(chosen[r][q][:4], row_of[r], value)
                out[p, q] = value

        for n in range(2):
            for core in range(2):
                forward(n, core).wait_send()

        @pl.when(c == 0)
        def _():
            for core in range(2):
                forward(2, core).wait_send()

        for t in range(1, 4):
            across(t).wait_send()
        for n in range(3):

            @pl.when(mine == n)
            def _():
                gone = last.at[0 : 19 - n]
                pltpu.make_async_copy(gone, gone, z_send).wait()


def local(spectra, model_corr, window_start, window_end, station_slot):
    angles = angle_parts()
    hbm = pl.BlockSpec(memory_space=pl.ANY)
    dma = pltpu.SemaphoreType.DMA
    return pl.pallas_call(
        kernel,
        out_shape=pltpu.VMEM((2, 4, 4, 128), F32),
        in_specs=[hbm] * 6,
        out_specs=pl.BlockSpec(memory_space=pltpu.VMEM),
        scratch_shapes=[
            pltpu.SMEM((1, 4), jnp.int32),
            pltpu.SMEM((1, 4), jnp.int32),
            pltpu.SMEM((1, 4), jnp.int32),
            pltpu.VMEM((2, 4, 4, 1024), BF16),
            pltpu.VMEM((1, 4, 4, 4, 1024), BF16),
            pltpu.VMEM((2, 160, 1024), F32),
            pltpu.VMEM((256, 128), F32),
            pltpu.VMEM((2, 128, 128), F32),
            pltpu.VMEM((2, 128, 128), BF16),
            pltpu.VMEM((128, 128), BF16),
            pltpu.VMEM((2, 256, 128), F32),
            pltpu.VMEM((5, 128, 128), BF16),
            pltpu.VMEM((512, 128), F32),
            pltpu.VMEM((2, 64, 1024), BF16),
            pltpu.VMEM((64, 1024), BF16),
            pltpu.VMEM((2, 1024, 1024), BF16),
            pltpu.VMEM((2, 1024, 1024), BF16),
            pltpu.VMEM((64, 1024), F32),
            pltpu.VMEM((64, 1024), F32),
            pltpu.VMEM((64, 1024), BF16),
            pltpu.VMEM((2, 64, 1024), BF16),
            pltpu.VMEM((64, 1024), BF16),
            pltpu.VMEM((2, 512, 128), F32),
            pltpu.VMEM((2, 256, 128), F32),
            pltpu.VMEM((2, 4, 128, 128), F32),
            pltpu.VMEM((4, 7, 32, 128), BF16),
            pltpu.VMEM((4, 7, 32, 128), BF16),
            pltpu.VMEM((5, 32, 128), BF16),
            pltpu.VMEM((20, 32, 128), BF16),
            dma((6,)), pltpu.SemaphoreType.REGULAR((5,)), dma((3,)), dma((3,)), dma((6,)), dma((5,)), dma((3,)), dma((4,)), dma, dma,
        ],
        compiler_params=pltpu.CompilerParams(has_side_effects=True, collective_id=0),
        name="adjoint",
    )(
        window_start, window_end, station_slot, spectra, model_corr, jnp.asarray(angles),
    )


def solution(mesh):
    in_specs = (
        P(None, "blk", None, None),
        P("blk", "lay", None, None, None),
        P("blk", "lay"),
        P("blk", "lay"),
        P("blk", None),
    )
    out_specs = P(None, "blk", None, "lay")
    return jax.shard_map(local, mesh=mesh, in_specs=in_specs, out_specs=out_specs, check_vma=False)
```

```python
import math

import jax
import jax.numpy as jnp
import numpy as np
from jax import lax
from jax.experimental import pallas as pl
from jax.experimental.pallas import tpu as pltpu
from jax.sharding import PartitionSpec as P

MESH = pl.DeviceIdType.MESH
F32 = jnp.float32
BF16 = jnp.bfloat16

SOURCE = [[3, 1, 0, 0, 0], [2, 0, 1, 1, 1], [3, 2, 2, 2, 1], [3, 3, 0, 3, 2]]
AHEAD = [[0, 0, 1, 1, 2], [2, 2, 3, 3, -4], [4, 4, -3, -3, -2], [-2, -2, -1, -1, 0]]
SENT = [
    [
        sorted(
            [(x, q) for x in range(4) for q in range(core, 5, 2) if SOURCE[x][q] == source],
            key=lambda to: -abs(AHEAD[to[0]][to[1]]),
        )
        for core in range(2)
    ]
    for source in range(4)
]


def angle_parts():
    lag = np.arange(1024, dtype=np.int64) - 512
    coarse = (np.arange(64, dtype=np.int64)[:, None] * 16 * lag[None]) % 2048
    fine = (np.arange(16, dtype=np.int64)[:, None] * lag[None]) % 2048
    scale = 1.0 / math.sqrt(8192.0)
    coarse = coarse * (math.pi / 1024)
    fine = fine * (math.pi / 1024)
    top = np.concatenate([np.cos(coarse), -np.sin(coarse)]) * scale
    low = np.concatenate([np.cos(fine), -np.sin(fine)])
    freq = np.arange(1024, dtype=np.int64)
    coarse = ((np.arange(64, dtype=np.int64)[:, None] * 16 - 512) * freq[None]) % 2048
    fine = (np.arange(16, dtype=np.int64)[:, None] * freq[None]) % 2048
    coarse = coarse * (math.pi / 1024)
    fine = fine * (math.pi / 1024)
    top2 = np.concatenate([np.cos(coarse), -np.sin(coarse)]) * scale
    low2 = np.concatenate([np.cos(fine), -np.sin(fine)])
    both = np.stack([np.concatenate([top, low]), np.concatenate([top2, low2])])
    return both.astype(np.float32)


def choose(index, values):
    result = jnp.int32(values[0])
    for n in range(1, len(values)):
        result = jnp.where(index == n, jnp.int32(values[n]), result)
    return result


def kernel(
    starts_hbm, ends_hbm, slots_hbm, spec_hbm, model_hbm, angles_hbm, out,
    starts, ends, slots, spec, model, angles, raw, halves, ordered, peer_half, first, partner, cross, left, left_out,
    table, turned, model_rows, lagged, misfit, resp, resp_out, resp_rows, own, part, outbox, inbox, merged, last,
    load_sem, ring_sem, peer_send, peer_recv, go_sem, come_sem, x_send, x_recv, z_send, z_recv,
):
    blk = lax.axis_index("blk")
    lay = lax.axis_index("lay")
    x = lax.rem(lay, 4)
    y = lax.div(blk, 16)
    zl = lax.div(lax.rem(blk, 16), 2)
    zh = lax.div(lay, 4)
    z = zh * 8 + zl
    c = lax.rem(blk, 2)
    other = 1 - c

    def device(x1, y1, z1, c1):
        return lax.rem(y1 + 8, 4) * 16 + lax.rem(z1, 8) * 2 + c1, lax.div(z1, 8) * 4 + x1

    peer = device(x, y, z, other)

    def receiver(n, core):
        to_x = jnp.where(
            c == 0,
            choose(x, [SENT[s][0][n][0] for s in range(4)]),
            choose(x, [SENT[s][1][min(n, 1)][0] for s in range(4)]),
        )
        q = jnp.where(
            c == 0,
            choose(x, [SENT[s][0][n][1] for s in range(4)]),
            choose(x, [SENT[s][1][min(n, 1)][1] for s in range(4)]),
        )
        ahead = jnp.where(
            c == 0,
            choose(x, [AHEAD[a][b] for a, b in (SENT[s][0][n] for s in range(4))]),
            choose(x, [AHEAD[a][b] for a, b in (SENT[s][1][min(n, 1)] for s in range(4))]),
        )
        to_z = lax.rem(z - ahead + 16, 16)
        to_y = y - lax.div(to_z + 2 * to_x + lax.div(q, 2), 8)
        return device(to_x, to_y, to_z, core), q

    def sender(q):
        from_z = lax.rem(z + choose(x, [AHEAD[s][q] for s in range(4)]) + 16, 16)
        from_y = y + lax.div(z + 2 * x + q // 2, 8)
        return device(choose(x, [SOURCE[s][q] for s in range(4)]), from_y, from_z, q % 2)

    mine = jnp.where(c == zh, 1, 0) + jnp.where((c == 0) & (zh == 0), 1, 0)

    def target(m):
        if isinstance(m, int) and m >= 17:
            return (16 * y + 2 * zl + m - 17, c * 4 + x), 16 + zh
        slot = lax.div(m, 2) * 2 + zh + (2 if isinstance(m, int) and m == 16 else 0)
        return (lax.rem(16 * y + 2 * z + m, 64), c * 4 + x), slot

    def elsewhere(to):
        return (to[0] != blk) | (to[1] != lay)

    with jax.named_scope("p00greet"):
        barrier = pltpu.get_barrier_semaphore()

        def greet(to):
            pl.semaphore_signal(barrier, inc=1, device_id=to, device_id_type=MESH)

        for q in range(5):
            greet(sender(q))
        greet(peer)
        for t in range(1, 4):
            greet((blk, zh * 4 + lax.rem(x + t, 4)))
        for d in (-4, -3, -2, -1, 1, 2, 3, 4):
            greet(device(x, y, lax.rem(z + d + 16, 16), c))
        for d in (1, 2, 3):
            greet(device(x, y + d, z, c))

    loads = [
        pltpu.make_async_copy(spec_hbm, spec, load_sem.at[0]),
        pltpu.make_async_copy(slots_hbm, slots, load_sem.at[1]),
        pltpu.make_async_copy(angles_hbm, angles, load_sem.at[2]),
        pltpu.make_async_copy(model_hbm, model, load_sem.at[3]),
        pltpu.make_async_copy(starts_hbm, starts, load_sem.at[4]),
        pltpu.make_async_copy(ends_hbm, ends, load_sem.at[5]),
    ]
    for load in loads:
        load.start()

    near = [
        [peer],
        [device(x, y + d, z, c) for d in (1, 2, 3)],
        [device(x, y, lax.rem(z + d + 16, 16), c) for d in (-4, 4)],
    ]

    def tell(n):
        for to in near[n]:
            pl.semaphore_signal(ring_sem.at[n], inc=1, device_id=to, device_id_type=MESH)

    def told(n):
        pl.semaphore_wait(ring_sem.at[n], len(near[n]))

    with jax.named_scope("p01order"):
        loads[0].wait()
        loads[1].wait()
        for n in range(8):
            value = spec[n // 4, n % 4].astype(F32)
            for k in range(8):
                raw[pl.ds(n * 32 + k, 4, stride=8), :] = value[:, k * 128 : (k + 1) * 128]
        slot_of = [jnp.full((8, 128), slots[0, r], jnp.int32) for r in range(4)]
        chosen = [[slot_of[r] == q for q in range(4)] for r in range(4)]
        for p in range(2):
            for r in range(4):
                for w in range(4):
                    value = jnp.zeros((8, 128), F32)
                    for q in range(4):
                        at = (p * 4 + q) * 32 + w * 8
                        value = jnp.where(chosen[r][q], raw[at : at + 8, :], value)
                    at = ((p * 4 + w) * 4 + r) * 4
                    halves[0, at : at + 4, :] = value[:4]
                    halves[1, at : at + 4, :] = value[4:]
        for h in range(2):
            ordered[h] = halves[h].astype(BF16)

    with jax.named_scope("p02barrier"):
        pl.semaphore_wait(barrier, 15 + 6 - 2 * c)

    peer_copy = pltpu.make_async_remote_copy(
        src_ref=ordered.at[other],
        dst_ref=peer_half,
        send_sem=peer_send.at[0],
        recv_sem=peer_recv.at[0],
        device_id=peer,
        device_id_type=MESH,
    )

    def forward(n, core):
        to, q = receiver(n, core)
        return pltpu.make_async_remote_copy(
            src_ref=ordered.at[core],
            dst_ref=partner.at[q],
            send_sem=go_sem.at[2 * n + core],
            recv_sem=come_sem.at[q],
            device_id=to,
            device_id_type=MESH,
        )

    with jax.named_scope("p03fwd"):
        for n in range(2):
            for core in range(2):
                forward(n, core).start()

        @pl.when(c == 0)
        def _():
            for core in range(2):
                forward(2, core).start()

        peer_copy.start()
        tell(0)

    with jax.named_scope("p04table"):
        loads[2].wait()

        @pl.loop(0, 64)
        def _(n):
            h = lax.div(n, 32)
            at_row = pl.multiple_of(lax.rem(n, 32) * 16, 16)
            for q in range(4):
                at = slice(q * 256, (q + 1) * 256)
                cos_top = angles[0, pl.ds(n, 1), at]
                sin_top = angles[0, pl.ds(64 + n, 1), at]
                cos_low = angles[0, 128:144, at]
                sin_low = angles[0, 144:160, at]
                table[h, pl.ds(at_row, 16), at] = (cos_top * cos_low - sin_top * sin_low).astype(BF16)
                table[h, pl.ds(512 + at_row, 16), at] = (sin_top * cos_low + cos_top * sin_low).astype(BF16)

        told(0)
        tell(1)

        @pl.loop(0, 64)
        def _(n):
            at_row = pl.multiple_of(n * 16, 16)
            for q in range(4):
                at = slice(q * 256, (q + 1) * 256)
                to = slice((q % 2) * 256, (q % 2) * 256 + 256)
                to_sin = slice(512 + (q % 2) * 256, 512 + (q % 2) * 256 + 256)
                cos_top = angles[1, pl.ds(n, 1), at]
                sin_top = angles[1, pl.ds(64 + n, 1), at]
                cos_low = angles[1, 128:144, at]
                sin_low = angles[1, 144:160, at]
                turned[q // 2, pl.ds(at_row, 16), to] = (cos_top * cos_low - sin_top * sin_low).astype(BF16)
                turned[q // 2, pl.ds(at_row, 16), to_sin] = (sin_top * cos_low + cos_top * sin_low).astype(BF16)

        told(1)
        tell(2)
        loads[3].wait()
        for n in range(16):
            model_rows[n * 4 : (n + 1) * 4, :] = model[0, n // 4, n % 4].astype(F32)

        peer_copy.wait()
        for t in range(2):
            source = jnp.where(t == c, halves[c], peer_half[...].astype(F32))
            raw[0:128, :] = source
            for n in range(32):
                value = raw[n * 4 : n * 4 + 4, :]
                first[t, n * 8 : n * 8 + 4, :] = value
                first[t, n * 8 + 4 : n * 8 + 8, :] = value

    with jax.named_scope("p05fwdwait"):
        for q in range(5):
            pltpu.make_async_copy(partner.at[q], partner.at[q], come_sem.at[q]).wait()

    def cross_of(t):
        @pl.loop(0, 4)
        def _(s):
            re = [None] * 8
            im = [None] * 8
            for w in range(4):
                u = [
                    first[t, ((p * 4 + w) * 4 + i) * 8 : ((p * 4 + w) * 4 + i) * 8 + 8, :]
                    for p in range(2)
                    for i in range(4)
                ]
                v_re = partner[t + s, w * 16 : w * 16 + 16, :].astype(F32)
                v_im = partner[t + s, 64 + w * 16 : 64 + w * 16 + 16, :].astype(F32)
                for i in range(4):
                    for jp in range(2):
                        a_re = v_re[jp * 8 : jp * 8 + 8]
                        a_im = v_im[jp * 8 : jp * 8 + 8]
                        a = u[i] * a_re + u[4 + i] * a_im
                        b = u[4 + i] * a_re - u[i] * a_im
                        n = i * 2 + jp
                        re[n] = a if w == 0 else re[n] + a
                        im[n] = b if w == 0 else im[n] + b
            for n in range(8):
                at = pl.multiple_of(s * 64 + n * 8, 8)
                cross[pl.ds(at, 8), :] = re[n]
                cross[pl.ds(256 + at, 8), :] = im[n]

    def gather(into):
        for h in range(2):
            for k in range(4):
                into[:, h * 512 + k * 128 : h * 512 + (k + 1) * 128] = cross[
                    pl.ds(h * 256 + k, 64, stride=4), :
                ].astype(BF16)

    left_copy = pltpu.make_async_remote_copy(
        src_ref=left_out,
        dst_ref=left.at[1],
        send_sem=peer_send.at[1],
        recv_sem=peer_recv.at[1],
        device_id=peer,
        device_id_type=MESH,
    )
    with jax.named_scope("p06cross"):
        cross_of(other)
        gather(left_out)
        left_copy.start()
        cross_of(c)
        gather(left.at[0])

    with jax.named_scope("p07lag"):
        lagged[...] = jnp.dot(left[0], table[c], preferred_element_type=F32)

        loads[4].wait()
        loads[5].wait()
        row = lax.broadcasted_iota(jnp.int32, (64, 1), 0)
        offset = lax.div(row, 16)
        start = jnp.zeros((64, 1), jnp.int32)
        end = jnp.zeros((64, 1), jnp.int32)
        for s in range(4):
            start = jnp.where(offset == s, starts[0, s], start)
            end = jnp.where(offset == s, ends[0, s], end)
        diagonal = (lax.rem(lax.div(row, 4), 4) == lax.rem(row, 4)) & (offset == 0) & (lay == 0)
        end = jnp.where(diagonal, 0, end)
        left_copy.wait()
        value = lagged[...] + jnp.dot(left[1], table[other], preferred_element_type=F32)
        lag = lax.broadcasted_iota(jnp.int32, (64, 1024), 1)
        keep = (lag >= start) & (lag < end)
        misfit[...] = jnp.where(keep, value - model_rows[...], 0.0).astype(BF16)

    resp_copy = pltpu.make_async_remote_copy(
        src_ref=resp_out,
        dst_ref=resp.at[1],
        send_sem=peer_send.at[2],
        recv_sem=peer_recv.at[2],
        device_id=peer,
        device_id_type=MESH,
    )

    def respond(h, into):
        into[...] = jnp.dot(misfit[...], turned[h], preferred_element_type=F32).astype(BF16)

    def spread(n, t):
        for p in range(2):
            for k in range(4):
                resp_rows[t, pl.ds(p * 256 + k, 64, stride=4), :] = resp[
                    n, :, p * 512 + k * 128 : p * 512 + (k + 1) * 128
                ].astype(F32)

    def terms_of(t):
        @pl.loop(0, 4)
        def _(w):
            at_u = [pl.multiple_of(((p * 4 + w) * 4) * 8, 8) for p in range(2)]
            at_v = [pl.multiple_of((p * 4 + w) * 16, 16) for p in range(2)]
            u = [first[t, pl.ds(at_u[p] + i * 8, 8), :] for p in range(2) for i in range(4)]
            total = [jnp.zeros((8, 128), F32)] * 8
            for s in range(4):
                v = [partner[t + s, pl.ds(at_v[p], 16), :].astype(F32) for p in range(2)]
                for jp in range(2):
                    v_re = v[0][jp * 8 : jp * 8 + 8]
                    v_im = v[1][jp * 8 : jp * 8 + 8]
                    part_re = jnp.zeros((8, 128), F32)
                    part_im = jnp.zeros((8, 128), F32)
                    for i in range(4):
                        at = ((s * 4 + i) * 2 + jp) * 8
                        a = resp_rows[t, at : at + 8, :]
                        b = resp_rows[t, 256 + at : 256 + at + 8, :]
                        total[i] = total[i] + (a * v_re - b * v_im)
                        total[4 + i] = total[4 + i] + (a * v_im + b * v_re)
                        part_re = part_re + (a * u[i] + b * u[4 + i])
                        part_im = part_im + (a * u[4 + i] - b * u[i])
                    part[t, s, pl.ds(at_v[0] + jp * 8, 8), :] = part_re
                    part[t, s, pl.ds(at_v[1] + jp * 8, 8), :] = part_im
            for p in range(2):
                for i in range(4):
                    own[t, pl.ds(((p * 4 + i) * 4 + w) * 8, 8), :] = total[p * 4 + i]

    with jax.named_scope("p08resp"):

        @pl.when(c == 0)
        def _():
            respond(0, resp.at[0])
            respond(1, resp_out)
            resp_copy.start()

        @pl.when(c == 1)
        def _():
            respond(0, resp_out)
            resp_copy.start()
            respond(1, resp.at[0])

        spread(0, c)
        terms_of(c)
        resp_copy.wait()

    with jax.named_scope("p09terms"):
        spread(1, other)
        terms_of(other)

    with jax.named_scope("p10pack"):
        for k in range(4):
            for t in range(2):
                outbox[k, 5 + t] = (
                    own[t, pl.ds(k, 32, stride=8), :] + own[t, pl.ds(4 + k, 32, stride=8), :]
                ).astype(BF16)
            for q in range(5):
                value = [part[t, q - t, pl.ds(k, 32, stride=4), :] for t in range(2) if 0 <= q - t < 4]
                outbox[k, q] = (value[0] if len(value) == 1 else value[0] + value[1]).astype(BF16)

    def far(n, q):
        if q == 5:
            return c != zh
        ahead = 2 * n + q // 2
        steps = lax.rem(8 * c + lax.rem(z + ahead, 8) - z + 16, 16)
        return (steps > 4) & (steps < 12)

    def rows(ref, n, q):
        return ref.at[n, 5:7] if q == 5 else ref.at[n, q]

    def across(t, q):
        to = lax.rem(x + t, 4)
        return pltpu.make_async_remote_copy(
            src_ref=rows(outbox, to, q),
            dst_ref=rows(inbox, x, q),
            send_sem=x_send,
            recv_sem=x_recv.at[x, q],
            device_id=(blk, zh * 4 + to),
            device_id_type=MESH,
        )

    def here(n, q):
        return pltpu.make_async_copy(rows(inbox, n, q), rows(inbox, n, q), x_recv.at[n, q])

    def deliver(source, m):
        to, slot = target(m)

        def start():
            pltpu.make_async_remote_copy(
                src_ref=source,
                dst_ref=last.at[slot],
                send_sem=z_send,
                recv_sem=z_recv,
                device_id=to,
                device_id_type=MESH,
            ).start()

        if isinstance(m, int) and m in (0, 17, 18):
            away = elsewhere(to)
            pl.when(away)(start)

            @pl.when(jnp.logical_not(away))
            def _():
                pltpu.make_async_copy(source, last.at[slot], z_recv).start()
        else:
            start()

    def when_far(now, n, q):
        return pl.when(far(n, q) if now else jnp.logical_not(far(n, q)))

    with jax.named_scope("p11x"):
        for now in (True, False):
            for t in (2, 1, 3):
                for q in (5, 0, 1, 2, 3, 4):
                    when_far(now, x, q)(across(t, q).start)
        for q in range(6):
            pltpu.make_async_copy(rows(outbox, x, q), rows(inbox, x, q), x_recv.at[x, q]).start()
        told(2)

    for now in (True, False):
        with jax.named_scope("p12relay" + str(int(now))):
            for n in (0, 3, 1, 2):
                if n == 1:
                    @when_far(now, 0, 5)
                    def _():
                        for n in range(4):
                            here(n, 5).wait()
                        for t in range(2):
                            value = inbox[0, 5 + t].astype(F32)
                            for n in range(1, 4):
                                value = value + inbox[n, 5 + t].astype(F32)
                            merged[3 + t] = value.astype(BF16)
                            deliver(merged.at[3 + t], 17 + t)

                for q in {0: (0, 1, 2, 3), 3: (4, 3, 2, 1), 1: (1, 2, 3), 2: (3, 2, 1)}[n]:

                    @when_far(now, n, q)
                    def _():
                        here(n, q).wait()
                        deliver(inbox.at[n, q], 4 * n + q)

            for n in range(1, 4):

                @when_far(now, n, 0)
                def _():
                    here(n, 0).wait()
                    here(n - 1, 4).wait()
                    merged[n - 1] = (inbox[n, 0].astype(F32) + inbox[n - 1, 4].astype(F32)).astype(BF16)
                    deliver(merged.at[n - 1], 4 * n)

    with jax.named_scope("p13wait"):

        @pl.when(c == 0)
        def _():
            pltpu.make_async_copy(last, last, z_recv).wait()

        @pl.when(c == 1)
        def _():
            pltpu.make_async_copy(last.at[0:18], last.at[0:18], z_recv).wait()

    with jax.named_scope("p14sum"):
        total = last[0].astype(F32)
        for n in range(1, 16):
            total = total + last[n].astype(F32)
        scale = 1.0 / 16.0
        raw[32:64, :] = (last[16].astype(F32) + last[17].astype(F32)) * scale

        @pl.when(c == 0)
        def _():
            raw[0:32, :] = (total + last[18].astype(F32) + last[19].astype(F32)) * scale

        @pl.when(c == 1)
        def _():
            raw[0:32, :] = total * scale

        for p in range(2):
            row_of = [
                raw[pl.ds(p * 16 + r, 4, stride=4), :]
                + raw[32 + p * 16 + r * 4 : 32 + p * 16 + r * 4 + 4, :]
                for r in range(4)
            ]
            for q in range(4):
                value = jnp.zeros((4, 128), F32)
                for r in range(4):
                    value = jnp.where(chosen[r][q][:4], row_of[r], value)
                out[p, q] = value

        for n in range(2):
            for core in range(2):
                forward(n, core).wait_send()

        @pl.when(c == 0)
        def _():
            for core in range(2):
                forward(2, core).wait_send()

        pltpu.make_async_copy(outbox.at[0:3], outbox.at[0:3], x_send).wait()
        for n in range(3):

            @pl.when(mine == n)
            def _():
                gone = last.at[0 : 19 - n]
                pltpu.make_async_copy(gone, gone, z_send).wait()


def local(spectra, model_corr, window_start, window_end, station_slot):
    angles = angle_parts()
    hbm = pl.BlockSpec(memory_space=pl.ANY)
    dma = pltpu.SemaphoreType.DMA
    return pl.pallas_call(
        kernel,
        out_shape=pltpu.VMEM((2, 4, 4, 128), F32),
        in_specs=[hbm] * 6,
        out_specs=pl.BlockSpec(memory_space=pltpu.VMEM),
        scratch_shapes=[
            pltpu.SMEM((1, 4), jnp.int32),
            pltpu.SMEM((1, 4), jnp.int32),
            pltpu.SMEM((1, 4), jnp.int32),
            pltpu.VMEM((2, 4, 4, 1024), BF16),
            pltpu.VMEM((1, 4, 4, 4, 1024), BF16),
            pltpu.VMEM((2, 160, 1024), F32),
            pltpu.VMEM((256, 128), F32),
            pltpu.VMEM((2, 128, 128), F32),
            pltpu.VMEM((2, 128, 128), BF16),
            pltpu.VMEM((128, 128), BF16),
            pltpu.VMEM((2, 256, 128), F32),
            pltpu.VMEM((5, 128, 128), BF16),
            pltpu.VMEM((512, 128), F32),
            pltpu.VMEM((2, 64, 1024), BF16),
            pltpu.VMEM((64, 1024), BF16),
            pltpu.VMEM((2, 1024, 1024), BF16),
            pltpu.VMEM((2, 1024, 1024), BF16),
            pltpu.VMEM((64, 1024), F32),
            pltpu.VMEM((64, 1024), F32),
            pltpu.VMEM((64, 1024), BF16),
            pltpu.VMEM((2, 64, 1024), BF16),
            pltpu.VMEM((64, 1024), BF16),
            pltpu.VMEM((2, 512, 128), F32),
            pltpu.VMEM((2, 256, 128), F32),
            pltpu.VMEM((2, 4, 128, 128), F32),
            pltpu.VMEM((4, 7, 32, 128), BF16),
            pltpu.VMEM((4, 7, 32, 128), BF16),
            pltpu.VMEM((5, 32, 128), BF16),
            pltpu.VMEM((20, 32, 128), BF16),
            dma((6,)), pltpu.SemaphoreType.REGULAR((3,)), dma((3,)), dma((3,)), dma((6,)), dma((5,)), dma, dma((4, 6)), dma, dma,
        ],
        compiler_params=pltpu.CompilerParams(has_side_effects=True, collective_id=0),
        name="adjoint",
    )(
        window_start, window_end, station_slot, spectra, model_corr, jnp.asarray(angles),
    )


def solution(mesh):
    in_specs = (
        P(None, "blk", None, None),
        P("blk", "lay", None, None, None),
        P("blk", "lay"),
        P("blk", "lay"),
        P("blk", None),
    )
    out_specs = P(None, "blk", None, "lay")
    return jax.shard_map(local, mesh=mesh, in_specs=in_specs, out_specs=out_specs, check_vma=False)
```

```python
import math

import jax
import jax.numpy as jnp
import numpy as np
from jax import lax
from jax.experimental import pallas as pl
from jax.experimental.pallas import tpu as pltpu
from jax.sharding import PartitionSpec as P

MESH = pl.DeviceIdType.MESH
F32 = jnp.float32
BF16 = jnp.bfloat16

SOURCE = [[3, 1, 0, 0, 0], [2, 0, 1, 1, 1], [3, 2, 2, 2, 1], [3, 3, 0, 3, 2]]
AHEAD = [[0, 0, 1, 1, 2], [2, 2, 3, 3, -4], [4, 4, -3, -3, -2], [-2, -2, -1, -1, 0]]
SENT = [
    [
        sorted(
            [(x, q) for x in range(4) for q in range(core, 5, 2) if SOURCE[x][q] == source],
            key=lambda to: -abs(AHEAD[to[0]][to[1]]),
        )
        for core in range(2)
    ]
    for source in range(4)
]


def angle_parts():
    lag = np.arange(1024, dtype=np.int64) - 512
    coarse = (np.arange(64, dtype=np.int64)[:, None] * 16 * lag[None]) % 2048
    fine = (np.arange(16, dtype=np.int64)[:, None] * lag[None]) % 2048
    scale = 1.0 / math.sqrt(8192.0)
    coarse = coarse * (math.pi / 1024)
    fine = fine * (math.pi / 1024)
    top = np.concatenate([np.cos(coarse), -np.sin(coarse)]) * scale
    low = np.concatenate([np.cos(fine), -np.sin(fine)])
    freq = np.arange(1024, dtype=np.int64)
    coarse = ((np.arange(64, dtype=np.int64)[:, None] * 16 - 512) * freq[None]) % 2048
    fine = (np.arange(16, dtype=np.int64)[:, None] * freq[None]) % 2048
    coarse = coarse * (math.pi / 1024)
    fine = fine * (math.pi / 1024)
    top2 = np.concatenate([np.cos(coarse), -np.sin(coarse)]) * scale
    low2 = np.concatenate([np.cos(fine), -np.sin(fine)])
    both = np.stack([np.concatenate([top, low]), np.concatenate([top2, low2])])
    return both.astype(np.float32)


def choose(index, values):
    result = jnp.int32(values[0])
    for n in range(1, len(values)):
        result = jnp.where(index == n, jnp.int32(values[n]), result)
    return result


def kernel(
    starts_hbm, ends_hbm, slots_hbm, spec_hbm, model_hbm, angles_hbm, out,
    starts, ends, slots, spec, model, angles, raw, halves, ordered, peer_half, first, partner, cross, left, left_out,
    table, turned, model_rows, lagged, misfit, resp, resp_out, resp_rows, own, part, outbox, inbox, merged, last,
    load_sem, ring_sem, peer_send, peer_recv, go_sem, come_sem, x_send, x_recv, z_send, z_recv,
):
    blk = lax.axis_index("blk")
    lay = lax.axis_index("lay")
    x = lax.rem(lay, 4)
    y = lax.div(blk, 16)
    zl = lax.div(lax.rem(blk, 16), 2)
    zh = lax.div(lay, 4)
    z = zh * 8 + zl
    c = lax.rem(blk, 2)
    other = 1 - c

    def device(x1, y1, z1, c1):
        return lax.rem(y1 + 8, 4) * 16 + lax.rem(z1, 8) * 2 + c1, lax.div(z1, 8) * 4 + x1

    peer = device(x, y, z, other)

    def receiver(n, core):
        to_x = jnp.where(
            c == 0,
            choose(x, [SENT[s][0][n][0] for s in range(4)]),
            choose(x, [SENT[s][1][min(n, 1)][0] for s in range(4)]),
        )
        q = jnp.where(
            c == 0,
            choose(x, [SENT[s][0][n][1] for s in range(4)]),
            choose(x, [SENT[s][1][min(n, 1)][1] for s in range(4)]),
        )
        ahead = jnp.where(
            c == 0,
            choose(x, [AHEAD[a][b] for a, b in (SENT[s][0][n] for s in range(4))]),
            choose(x, [AHEAD[a][b] for a, b in (SENT[s][1][min(n, 1)] for s in range(4))]),
        )
        to_z = lax.rem(z - ahead + 16, 16)
        to_y = y - lax.div(to_z + 2 * to_x + lax.div(q, 2), 8)
        return device(to_x, to_y, to_z, core), q

    def sender(q):
        from_z = lax.rem(z + choose(x, [AHEAD[s][q] for s in range(4)]) + 16, 16)
        from_y = y + lax.div(z + 2 * x + q // 2, 8)
        return device(choose(x, [SOURCE[s][q] for s in range(4)]), from_y, from_z, q % 2)

    mine = jnp.where(c == zh, 1, 0) + jnp.where((c == 0) & (zh == 0), 1, 0)

    def target(m):
        if isinstance(m, int) and m >= 17:
            return (16 * y + 2 * zl + m - 17, c * 4 + x), 16 + zh
        slot = lax.div(m, 2) * 2 + zh + (2 if isinstance(m, int) and m == 16 else 0)
        return (lax.rem(16 * y + 2 * z + m, 64), c * 4 + x), slot

    def elsewhere(to):
        return (to[0] != blk) | (to[1] != lay)

    with jax.named_scope("p00greet"):
        barrier = pltpu.get_barrier_semaphore()

        def greet(to):
            pl.semaphore_signal(barrier, inc=1, device_id=to, device_id_type=MESH)

        for q in range(5):
            greet(sender(q))
        greet(peer)
        for t in range(1, 4):
            greet((blk, zh * 4 + lax.rem(x + t, 4)))
        for d in (-4, -3, -2, -1, 1, 2, 3, 4):
            greet(device(x, y, lax.rem(z + d + 16, 16), c))
        for d in (1, 2, 3):
            greet(device(x, y + d, z, c))

    loads = [
        pltpu.make_async_copy(spec_hbm, spec, load_sem.at[0]),
        pltpu.make_async_copy(slots_hbm, slots, load_sem.at[1]),
        pltpu.make_async_copy(angles_hbm, angles, load_sem.at[2]),
        pltpu.make_async_copy(model_hbm, model, load_sem.at[3]),
        pltpu.make_async_copy(starts_hbm, starts, load_sem.at[4]),
        pltpu.make_async_copy(ends_hbm, ends, load_sem.at[5]),
    ]
    for load in loads:
        load.start()

    near = [
        [peer],
        [device(x, y + d, z, c) for d in (1, 2, 3)],
        [device(x, y, lax.rem(z + d + 16, 16), c) for d in (-4, 4)],
    ]

    def tell(n):
        for to in near[n]:
            pl.semaphore_signal(ring_sem.at[n], inc=1, device_id=to, device_id_type=MESH)

    def told(n):
        pl.semaphore_wait(ring_sem.at[n], len(near[n]))

    with jax.named_scope("p01order"):
        loads[0].wait()
        loads[1].wait()
        for n in range(8):
            value = spec[n // 4, n % 4].astype(F32)
            for k in range(8):
                raw[pl.ds(n * 32 + k, 4, stride=8), :] = value[:, k * 128 : (k + 1) * 128]
        slot_of = [jnp.full((8, 128), slots[0, r], jnp.int32) for r in range(4)]
        chosen = [[slot_of[r] == q for q in range(4)] for r in range(4)]
        for p in range(2):
            for r in range(4):
                for w in range(4):
                    value = jnp.zeros((8, 128), F32)
                    for q in range(4):
                        at = (p * 4 + q) * 32 + w * 8
                        value = jnp.where(chosen[r][q], raw[at : at + 8, :], value)
                    at = ((p * 4 + w) * 4 + r) * 4
                    halves[0, at : at + 4, :] = value[:4]
                    halves[1, at : at + 4, :] = value[4:]
        for h in range(2):
            ordered[h] = halves[h].astype(BF16)

    with jax.named_scope("p02barrier"):
        pl.semaphore_wait(barrier, 15 + 6 - 2 * c)

    peer_copy = pltpu.make_async_remote_copy(
        src_ref=ordered.at[other],
        dst_ref=peer_half,
        send_sem=peer_send.at[0],
        recv_sem=peer_recv.at[0],
        device_id=peer,
        device_id_type=MESH,
    )

    def forward(n, core):
        to, q = receiver(n, core)
        return pltpu.make_async_remote_copy(
            src_ref=ordered.at[core],
            dst_ref=partner.at[q],
            send_sem=go_sem,
            recv_sem=come_sem,
            device_id=to,
            device_id_type=MESH,
        )

    with jax.named_scope("p03fwd"):
        for n in range(2):
            for core in range(2):
                forward(n, core).start()

        @pl.when(c == 0)
        def _():
            for core in range(2):
                forward(2, core).start()

        peer_copy.start()
        tell(0)

    with jax.named_scope("p04table"):
        loads[2].wait()

        @pl.loop(0, 64)
        def _(n):
            h = lax.div(n, 32)
            at_row = pl.multiple_of(lax.rem(n, 32) * 16, 16)
            for q in range(4):
                at = slice(q * 256, (q + 1) * 256)
                cos_top = angles[0, pl.ds(n, 1), at]
                sin_top = angles[0, pl.ds(64 + n, 1), at]
                cos_low = angles[0, 128:144, at]
                sin_low = angles[0, 144:160, at]
                table[h, pl.ds(at_row, 16), at] = (cos_top * cos_low - sin_top * sin_low).astype(BF16)
                table[h, pl.ds(512 + at_row, 16), at] = (sin_top * cos_low + cos_top * sin_low).astype(BF16)

        told(0)
        tell(1)

        @pl.loop(0, 64)
        def _(n):
            at_row = pl.multiple_of(n * 16, 16)
            for q in range(4):
                at = slice(q * 256, (q + 1) * 256)
                to = slice((q % 2) * 256, (q % 2) * 256 + 256)
                to_sin = slice(512 + (q % 2) * 256, 512 + (q % 2) * 256 + 256)
                cos_top = angles[1, pl.ds(n, 1), at]
                sin_top = angles[1, pl.ds(64 + n, 1), at]
                cos_low = angles[1, 128:144, at]
                sin_low = angles[1, 144:160, at]
                turned[q // 2, pl.ds(at_row, 16), to] = (cos_top * cos_low - sin_top * sin_low).astype(BF16)
                turned[q // 2, pl.ds(at_row, 16), to_sin] = (sin_top * cos_low + cos_top * sin_low).astype(BF16)

        told(1)
        tell(2)
        loads[3].wait()
        for n in range(16):
            model_rows[n * 4 : (n + 1) * 4, :] = model[0, n // 4, n % 4].astype(F32)

        peer_copy.wait()
        for t in range(2):
            source = jnp.where(t == c, halves[c], peer_half[...].astype(F32))
            raw[0:128, :] = source
            for n in range(32):
                value = raw[n * 4 : n * 4 + 4, :]
                first[t, n * 8 : n * 8 + 4, :] = value
                first[t, n * 8 + 4 : n * 8 + 8, :] = value

    with jax.named_scope("p05fwdwait"):
        pltpu.make_async_copy(partner, partner, come_sem).wait()

    def cross_of(t):
        @pl.loop(0, 4)
        def _(s):
            re = [None] * 8
            im = [None] * 8
            for w in range(4):
                u = [
                    first[t, ((p * 4 + w) * 4 + i) * 8 : ((p * 4 + w) * 4 + i) * 8 + 8, :]
                    for p in range(2)
                    for i in range(4)
                ]
                v_re = partner[t + s, w * 16 : w * 16 + 16, :].astype(F32)
                v_im = partner[t + s, 64 + w * 16 : 64 + w * 16 + 16, :].astype(F32)
                for i in range(4):
                    for jp in range(2):
                        a_re = v_re[jp * 8 : jp * 8 + 8]
                        a_im = v_im[jp * 8 : jp * 8 + 8]
                        a = u[i] * a_re + u[4 + i] * a_im
                        b = u[4 + i] * a_re - u[i] * a_im
                        n = i * 2 + jp
                        re[n] = a if w == 0 else re[n] + a
                        im[n] = b if w == 0 else im[n] + b
            for n in range(8):
                at = pl.multiple_of(s * 64 + n * 8, 8)
                cross[pl.ds(at, 8), :] = re[n]
                cross[pl.ds(256 + at, 8), :] = im[n]

    def gather(into):
        for h in range(2):
            for k in range(4):
                into[:, h * 512 + k * 128 : h * 512 + (k + 1) * 128] = cross[
                    pl.ds(h * 256 + k, 64, stride=4), :
                ].astype(BF16)

    left_copy = pltpu.make_async_remote_copy(
        src_ref=left_out,
        dst_ref=left.at[1],
        send_sem=peer_send.at[1],
        recv_sem=peer_recv.at[1],
        device_id=peer,
        device_id_type=MESH,
    )
    with jax.named_scope("p06cross"):
        cross_of(other)
        gather(left_out)
        left_copy.start()
        cross_of(c)
        gather(left.at[0])

    with jax.named_scope("p07lag"):
        lagged[...] = jnp.dot(left[0], table[c], preferred_element_type=F32)

        loads[4].wait()
        loads[5].wait()
        row = lax.broadcasted_iota(jnp.int32, (64, 1), 0)
        offset = lax.div(row, 16)
        start = jnp.zeros((64, 1), jnp.int32)
        end = jnp.zeros((64, 1), jnp.int32)
        for s in range(4):
            start = jnp.where(offset == s, starts[0, s], start)
            end = jnp.where(offset == s, ends[0, s], end)
        diagonal = (lax.rem(lax.div(row, 4), 4) == lax.rem(row, 4)) & (offset == 0) & (lay == 0)
        end = jnp.where(diagonal, 0, end)
        left_copy.wait()
        value = lagged[...] + jnp.dot(left[1], table[other], preferred_element_type=F32)
        lag = lax.broadcasted_iota(jnp.int32, (64, 1024), 1)
        keep = (lag >= start) & (lag < end)
        misfit[...] = jnp.where(keep, value - model_rows[...], 0.0).astype(BF16)

    resp_copy = pltpu.make_async_remote_copy(
        src_ref=resp_out,
        dst_ref=resp.at[1],
        send_sem=peer_send.at[2],
        recv_sem=peer_recv.at[2],
        device_id=peer,
        device_id_type=MESH,
    )

    def respond(h, into):
        into[...] = jnp.dot(misfit[...], turned[h], preferred_element_type=F32).astype(BF16)

    def spread(n, t):
        for p in range(2):
            for k in range(4):
                resp_rows[t, pl.ds(p * 256 + k, 64, stride=4), :] = resp[
                    n, :, p * 512 + k * 128 : p * 512 + (k + 1) * 128
                ].astype(F32)

    def terms_of(t):
        @pl.loop(0, 4)
        def _(w):
            at_u = [pl.multiple_of(((p * 4 + w) * 4) * 8, 8) for p in range(2)]
            at_v = [pl.multiple_of((p * 4 + w) * 16, 16) for p in range(2)]
            u = [first[t, pl.ds(at_u[p] + i * 8, 8), :] for p in range(2) for i in range(4)]
            total = [jnp.zeros((8, 128), F32)] * 8
            for s in range(4):
                v = [partner[t + s, pl.ds(at_v[p], 16), :].astype(F32) for p in range(2)]
                for jp in range(2):
                    v_re = v[0][jp * 8 : jp * 8 + 8]
                    v_im = v[1][jp * 8 : jp * 8 + 8]
                    part_re = jnp.zeros((8, 128), F32)
                    part_im = jnp.zeros((8, 128), F32)
                    for i in range(4):
                        at = ((s * 4 + i) * 2 + jp) * 8
                        a = resp_rows[t, at : at + 8, :]
                        b = resp_rows[t, 256 + at : 256 + at + 8, :]
                        total[i] = total[i] + (a * v_re - b * v_im)
                        total[4 + i] = total[4 + i] + (a * v_im + b * v_re)
                        part_re = part_re + (a * u[i] + b * u[4 + i])
                        part_im = part_im + (a * u[4 + i] - b * u[i])
                    part[t, s, pl.ds(at_v[0] + jp * 8, 8), :] = part_re
                    part[t, s, pl.ds(at_v[1] + jp * 8, 8), :] = part_im
            for p in range(2):
                for i in range(4):
                    own[t, pl.ds(((p * 4 + i) * 4 + w) * 8, 8), :] = total[p * 4 + i]

    with jax.named_scope("p08resp"):

        @pl.when(c == 0)
        def _():
            respond(0, resp.at[0])
            respond(1, resp_out)
            resp_copy.start()

        @pl.when(c == 1)
        def _():
            respond(0, resp_out)
            resp_copy.start()
            respond(1, resp.at[0])

        spread(0, c)
        terms_of(c)
        resp_copy.wait()

    with jax.named_scope("p09terms"):
        spread(1, other)
        terms_of(other)

    with jax.named_scope("p10pack"):
        for k in range(4):
            for t in range(2):
                outbox[k, 5 + t] = (
                    own[t, pl.ds(k, 32, stride=8), :] + own[t, pl.ds(4 + k, 32, stride=8), :]
                ).astype(BF16)
            for q in range(5):
                value = [part[t, q - t, pl.ds(k, 32, stride=4), :] for t in range(2) if 0 <= q - t < 4]
                outbox[k, q] = (value[0] if len(value) == 1 else value[0] + value[1]).astype(BF16)

    def across(t):
        to = lax.rem(x + t, 4)
        return pltpu.make_async_remote_copy(
            src_ref=outbox.at[to],
            dst_ref=inbox.at[x],
            send_sem=x_send,
            recv_sem=x_recv.at[x],
            device_id=(blk, zh * 4 + to),
            device_id_type=MESH,
        )

    def here(n):
        pltpu.make_async_copy(inbox.at[n], inbox.at[n], x_recv.at[n]).wait()

    def deliver(source, m):
        to, slot = target(m)

        def start():
            pltpu.make_async_remote_copy(
                src_ref=source,
                dst_ref=last.at[slot],
                send_sem=z_send,
                recv_sem=z_recv,
                device_id=to,
                device_id_type=MESH,
            ).start()

        if isinstance(m, int) and m in (0, 17, 18):
            away = elsewhere(to)
            pl.when(away)(start)

            @pl.when(jnp.logical_not(away))
            def _():
                pltpu.make_async_copy(source, last.at[slot], z_recv).start()
        else:
            start()

    with jax.named_scope("p11x"):
        for t in (2, 1, 3):
            across(t).start()
        pltpu.make_async_copy(outbox.at[x], inbox.at[x], x_recv.at[x]).start()
        told(2)

    def merge(n):
        merged[n - 1] = (inbox[n, 0].astype(F32) + inbox[n - 1, 4].astype(F32)).astype(BF16)
        deliver(merged.at[n - 1], 4 * n)

    with jax.named_scope("p12relay"):
        for n, single in ((0, (0, 1, 2, 3)), (3, (4, 3, 2, 1)), (1, (3, 2, 1)), (2, (3, 2, 1))):
            here(n)
            for q in single:
                deliver(inbox.at[n, q], 4 * n + q)
            if n == 1:
                merge(1)
        merge(3)
        merge(2)
        for t in range(2):
            value = inbox[0, 5 + t].astype(F32)
            for n in range(1, 4):
                value = value + inbox[n, 5 + t].astype(F32)
            merged[3 + t] = value.astype(BF16)
            deliver(merged.at[3 + t], 17 + t)

    with jax.named_scope("p13wait"):

        @pl.when(c == 0)
        def _():
            pltpu.make_async_copy(last, last, z_recv).wait()

        @pl.when(c == 1)
        def _():
            pltpu.make_async_copy(last.at[0:18], last.at[0:18], z_recv).wait()

    with jax.named_scope("p14sum"):
        total = last[0].astype(F32)
        for n in range(1, 16):
            total = total + last[n].astype(F32)
        scale = 1.0 / 16.0
        raw[32:64, :] = (last[16].astype(F32) + last[17].astype(F32)) * scale

        @pl.when(c == 0)
        def _():
            raw[0:32, :] = (total + last[18].astype(F32) + last[19].astype(F32)) * scale

        @pl.when(c == 1)
        def _():
            raw[0:32, :] = total * scale

        for p in range(2):
            row_of = [
                raw[pl.ds(p * 16 + r, 4, stride=4), :]
                + raw[32 + p * 16 + r * 4 : 32 + p * 16 + r * 4 + 4, :]
                for r in range(4)
            ]
            for q in range(4):
                value = jnp.zeros((4, 128), F32)
                for r in range(4):
                    value = jnp.where(chosen[r][q][:4], row_of[r], value)
                out[p, q] = value

        for half in range(2):

            @pl.when(c == half)
            def _():
                gone = table.at[0, 0 : 96 - 32 * half]
                pltpu.make_async_copy(gone, gone, go_sem).wait()

        pltpu.make_async_copy(outbox.at[0:3], outbox.at[0:3], x_send).wait()
        for n in range(3):

            @pl.when(mine == n)
            def _():
                gone = last.at[0 : 19 - n]
                pltpu.make_async_copy(gone, gone, z_send).wait()


def local(spectra, model_corr, window_start, window_end, station_slot):
    angles = angle_parts()
    hbm = pl.BlockSpec(memory_space=pl.ANY)
    dma = pltpu.SemaphoreType.DMA
    return pl.pallas_call(
        kernel,
        out_shape=pltpu.VMEM((2, 4, 4, 128), F32),
        in_specs=[hbm] * 6,
        out_specs=pl.BlockSpec(memory_space=pltpu.VMEM),
        scratch_shapes=[
            pltpu.SMEM((1, 4), jnp.int32),
            pltpu.SMEM((1, 4), jnp.int32),
            pltpu.SMEM((1, 4), jnp.int32),
            pltpu.VMEM((2, 4, 4, 1024), BF16),
            pltpu.VMEM((1, 4, 4, 4, 1024), BF16),
            pltpu.VMEM((2, 160, 1024), F32),
            pltpu.VMEM((256, 128), F32),
            pltpu.VMEM((2, 128, 128), F32),
            pltpu.VMEM((2, 128, 128), BF16),
            pltpu.VMEM((128, 128), BF16),
            pltpu.VMEM((2, 256, 128), F32),
            pltpu.VMEM((5, 128, 128), BF16),
            pltpu.VMEM((512, 128), F32),
            pltpu.VMEM((2, 64, 1024), BF16),
            pltpu.VMEM((64, 1024), BF16),
            pltpu.VMEM((2, 1024, 1024), BF16),
            pltpu.VMEM((2, 1024, 1024), BF16),
            pltpu.VMEM((64, 1024), F32),
            pltpu.VMEM((64, 1024), F32),
            pltpu.VMEM((64, 1024), BF16),
            pltpu.VMEM((2, 64, 1024), BF16),
            pltpu.VMEM((64, 1024), BF16),
            pltpu.VMEM((2, 512, 128), F32),
            pltpu.VMEM((2, 256, 128), F32),
            pltpu.VMEM((2, 4, 128, 128), F32),
            pltpu.VMEM((4, 7, 32, 128), BF16),
            pltpu.VMEM((4, 7, 32, 128), BF16),
            pltpu.VMEM((5, 32, 128), BF16),
            pltpu.VMEM((20, 32, 128), BF16),
            dma((6,)), pltpu.SemaphoreType.REGULAR((3,)), dma((3,)), dma((3,)), dma, dma, dma, dma((4,)), dma, dma,
        ],
        compiler_params=pltpu.CompilerParams(has_side_effects=True, collective_id=0),
        name="adjoint",
    )(
        window_start, window_end, station_slot, spectra, model_corr, jnp.asarray(angles),
    )


def solution(mesh):
    in_specs = (
        P(None, "blk", None, None),
        P("blk", "lay", None, None, None),
        P("blk", "lay"),
        P("blk", "lay"),
        P("blk", None),
    )
    out_specs = P(None, "blk", None, "lay")
    return jax.shard_map(local, mesh=mesh, in_specs=in_specs, out_specs=out_specs, check_vma=False)
```

```python
import math

import jax
import jax.numpy as jnp
import numpy as np
from jax import lax
from jax.experimental import pallas as pl
from jax.experimental.pallas import tpu as pltpu
from jax.sharding import PartitionSpec as P

MESH = pl.DeviceIdType.MESH
F32 = jnp.float32
BF16 = jnp.bfloat16

SOURCE = [[3, 1, 0, 0, 0], [2, 0, 1, 1, 1], [3, 2, 2, 2, 1], [3, 3, 0, 3, 2]]
AHEAD = [[0, 0, 1, 1, 2], [2, 2, 3, 3, -4], [4, 4, -3, -3, -2], [-2, -2, -1, -1, 0]]
SENT = [
    [
        sorted(
            [(x, q) for x in range(4) for q in range(core, 5, 2) if SOURCE[x][q] == source],
            key=lambda to: -abs(AHEAD[to[0]][to[1]]),
        )
        for core in range(2)
    ]
    for source in range(4)
]


def angle_parts():
    lag = np.arange(1024, dtype=np.int64) - 512
    coarse = (np.arange(64, dtype=np.int64)[:, None] * 16 * lag[None]) % 2048
    fine = (np.arange(16, dtype=np.int64)[:, None] * lag[None]) % 2048
    scale = 1.0 / math.sqrt(8192.0)
    coarse = coarse * (math.pi / 1024)
    fine = fine * (math.pi / 1024)
    top = np.concatenate([np.cos(coarse), -np.sin(coarse)]) * scale
    low = np.concatenate([np.cos(fine), -np.sin(fine)])
    freq = np.arange(1024, dtype=np.int64)
    coarse = ((np.arange(64, dtype=np.int64)[:, None] * 16 - 512) * freq[None]) % 2048
    fine = (np.arange(16, dtype=np.int64)[:, None] * freq[None]) % 2048
    coarse = coarse * (math.pi / 1024)
    fine = fine * (math.pi / 1024)
    top2 = np.concatenate([np.cos(coarse), -np.sin(coarse)]) * scale
    low2 = np.concatenate([np.cos(fine), -np.sin(fine)])
    both = np.stack([np.concatenate([top, low]), np.concatenate([top2, low2])])
    return both.astype(np.float32)


def choose(index, values):
    result = jnp.int32(values[0])
    for n in range(1, len(values)):
        result = jnp.where(index == n, jnp.int32(values[n]), result)
    return result


def kernel(
    starts_hbm, ends_hbm, slots_hbm, spec_hbm, model_hbm, angles_hbm, out,
    starts, ends, slots, spec, model, angles, raw, halves, ordered, peer_half, first, partner, cross, left, left_out,
    table, turned, model_rows, lagged, misfit, resp, resp_out, resp_rows, own, part, outbox, inbox, merged, last,
    load_sem, ring_sem, peer_send, peer_recv, go_sem, come_sem, x_send, x_recv, z_send, z_recv,
):
    blk = lax.axis_index("blk")
    lay = lax.axis_index("lay")
    x = lax.rem(lay, 4)
    y = lax.div(blk, 16)
    zl = lax.div(lax.rem(blk, 16), 2)
    zh = lax.div(lay, 4)
    z = zh * 8 + zl
    c = lax.rem(blk, 2)
    other = 1 - c

    def device(x1, y1, z1, c1):
        return lax.rem(y1 + 8, 4) * 16 + lax.rem(z1, 8) * 2 + c1, lax.div(z1, 8) * 4 + x1

    peer = device(x, y, z, other)

    def receiver(n, core):
        to_x = jnp.where(
            c == 0,
            choose(x, [SENT[s][0][n][0] for s in range(4)]),
            choose(x, [SENT[s][1][min(n, 1)][0] for s in range(4)]),
        )
        q = jnp.where(
            c == 0,
            choose(x, [SENT[s][0][n][1] for s in range(4)]),
            choose(x, [SENT[s][1][min(n, 1)][1] for s in range(4)]),
        )
        ahead = jnp.where(
            c == 0,
            choose(x, [AHEAD[a][b] for a, b in (SENT[s][0][n] for s in range(4))]),
            choose(x, [AHEAD[a][b] for a, b in (SENT[s][1][min(n, 1)] for s in range(4))]),
        )
        to_z = lax.rem(z - ahead + 16, 16)
        to_y = y - lax.div(to_z + 2 * to_x + lax.div(q, 2), 8)
        return device(to_x, to_y, to_z, core), q

    def sender(q):
        from_z = lax.rem(z + choose(x, [AHEAD[s][q] for s in range(4)]) + 16, 16)
        from_y = y + lax.div(z + 2 * x + q // 2, 8)
        return device(choose(x, [SOURCE[s][q] for s in range(4)]), from_y, from_z, q % 2)

    mine = jnp.where(c == zh, 1, 0) + jnp.where((c == 0) & (zh == 0) & (x != 2), 1, 0)
    over = lax.rem(x + 2, 4)
    outer = (x == 0) | (x == 3)

    def target(m):
        if isinstance(m, int) and m >= 17:
            return (16 * y + 2 * zl + m - 17, c * 4 + x), 16 + zh
        slot = lax.div(m, 2) * 2 + zh + (2 if isinstance(m, int) and m == 16 else 0)
        return (lax.rem(16 * y + 2 * z + m, 64), c * 4 + x), slot

    def elsewhere(to):
        return (to[0] != blk) | (to[1] != lay)

    with jax.named_scope("p00greet"):
        barrier = pltpu.get_barrier_semaphore()

        def greet(to):
            pl.semaphore_signal(barrier, inc=1, device_id=to, device_id_type=MESH)

        for q in range(5):
            greet(sender(q))
        greet(peer)
        for t in range(1, 4):
            greet((blk, zh * 4 + lax.rem(x + t, 4)))
        for d in (-4, -3, -2, -1, 1, 2, 3, 4):
            greet(device(x, y, lax.rem(z + d + 16, 16), c))
        for d in (1, 2, 3):
            greet(device(x, y + d, z, c))

    loads = [
        pltpu.make_async_copy(spec_hbm, spec, load_sem.at[0]),
        pltpu.make_async_copy(slots_hbm, slots, load_sem.at[1]),
        pltpu.make_async_copy(angles_hbm, angles, load_sem.at[2]),
        pltpu.make_async_copy(model_hbm, model, load_sem.at[3]),
        pltpu.make_async_copy(starts_hbm, starts, load_sem.at[4]),
        pltpu.make_async_copy(ends_hbm, ends, load_sem.at[5]),
    ]
    for load in loads:
        load.start()

    near = [
        [peer],
        [device(x, y + d, z, c) for d in (1, 2, 3)],
        [device(x, y, lax.rem(z + d + 16, 16), c) for d in (-4, 4)],
        [device(lax.rem(x + 2, 4), y, z, c)],
    ]

    def tell(n):
        for to in near[n]:
            pl.semaphore_signal(ring_sem.at[n], inc=1, device_id=to, device_id_type=MESH)

    def told(n):
        pl.semaphore_wait(ring_sem.at[n], len(near[n]))

    with jax.named_scope("p01order"):
        loads[0].wait()
        loads[1].wait()
        for n in range(8):
            value = spec[n // 4, n % 4].astype(F32)
            for k in range(8):
                raw[pl.ds(n * 32 + k, 4, stride=8), :] = value[:, k * 128 : (k + 1) * 128]
        slot_of = [jnp.full((8, 128), slots[0, r], jnp.int32) for r in range(4)]
        chosen = [[slot_of[r] == q for q in range(4)] for r in range(4)]
        for p in range(2):
            for r in range(4):
                for w in range(4):
                    value = jnp.zeros((8, 128), F32)
                    for q in range(4):
                        at = (p * 4 + q) * 32 + w * 8
                        value = jnp.where(chosen[r][q], raw[at : at + 8, :], value)
                    at = ((p * 4 + w) * 4 + r) * 4
                    halves[0, at : at + 4, :] = value[:4]
                    halves[1, at : at + 4, :] = value[4:]
        for h in range(2):
            ordered[h] = halves[h].astype(BF16)

    with jax.named_scope("p02barrier"):
        pl.semaphore_wait(barrier, 15 + 6 - 2 * c)

    peer_copy = pltpu.make_async_remote_copy(
        src_ref=ordered.at[other],
        dst_ref=peer_half,
        send_sem=peer_send.at[0],
        recv_sem=peer_recv.at[0],
        device_id=peer,
        device_id_type=MESH,
    )

    def forward(n, core):
        to, q = receiver(n, core)
        return pltpu.make_async_remote_copy(
            src_ref=ordered.at[core],
            dst_ref=partner.at[q],
            send_sem=go_sem,
            recv_sem=come_sem,
            device_id=to,
            device_id_type=MESH,
        )

    with jax.named_scope("p03fwd"):
        for n in range(2):
            for core in range(2):
                forward(n, core).start()

        @pl.when(c == 0)
        def _():
            for core in range(2):
                forward(2, core).start()

        peer_copy.start()
        tell(3)

    with jax.named_scope("p04table"):
        loads[2].wait()

        @pl.loop(0, 64)
        def _(n):
            h = lax.div(n, 32)
            at_row = pl.multiple_of(lax.rem(n, 32) * 16, 16)
            for q in range(4):
                at = slice(q * 256, (q + 1) * 256)
                cos_top = angles[0, pl.ds(n, 1), at]
                sin_top = angles[0, pl.ds(64 + n, 1), at]
                cos_low = angles[0, 128:144, at]
                sin_low = angles[0, 144:160, at]
                table[h, pl.ds(at_row, 16), at] = (cos_top * cos_low - sin_top * sin_low).astype(BF16)
                table[h, pl.ds(512 + at_row, 16), at] = (sin_top * cos_low + cos_top * sin_low).astype(BF16)

        told(3)
        tell(0)

        @pl.loop(0, 64)
        def _(n):
            at_row = pl.multiple_of(n * 16, 16)
            for q in range(4):
                at = slice(q * 256, (q + 1) * 256)
                to = slice((q % 2) * 256, (q % 2) * 256 + 256)
                to_sin = slice(512 + (q % 2) * 256, 512 + (q % 2) * 256 + 256)
                cos_top = angles[1, pl.ds(n, 1), at]
                sin_top = angles[1, pl.ds(64 + n, 1), at]
                cos_low = angles[1, 128:144, at]
                sin_low = angles[1, 144:160, at]
                turned[q // 2, pl.ds(at_row, 16), to] = (cos_top * cos_low - sin_top * sin_low).astype(BF16)
                turned[q // 2, pl.ds(at_row, 16), to_sin] = (sin_top * cos_low + cos_top * sin_low).astype(BF16)

        told(0)
        tell(1)
        loads[3].wait()
        for n in range(16):
            model_rows[n * 4 : (n + 1) * 4, :] = model[0, n // 4, n % 4].astype(F32)

        peer_copy.wait()
        for t in range(2):
            source = jnp.where(t == c, halves[c], peer_half[...].astype(F32))
            raw[0:128, :] = source
            for n in range(32):
                value = raw[n * 4 : n * 4 + 4, :]
                first[t, n * 8 : n * 8 + 4, :] = value
                first[t, n * 8 + 4 : n * 8 + 8, :] = value

        told(1)
        tell(2)

    with jax.named_scope("p05fwdwait"):
        pltpu.make_async_copy(partner, partner, come_sem).wait()

    def cross_of(t):
        @pl.loop(0, 4)
        def _(s):
            re = [None] * 8
            im = [None] * 8
            for w in range(4):
                u = [
                    first[t, ((p * 4 + w) * 4 + i) * 8 : ((p * 4 + w) * 4 + i) * 8 + 8, :]
                    for p in range(2)
                    for i in range(4)
                ]
                v_re = partner[t + s, w * 16 : w * 16 + 16, :].astype(F32)
                v_im = partner[t + s, 64 + w * 16 : 64 + w * 16 + 16, :].astype(F32)
                for i in range(4):
                    for jp in range(2):
                        a_re = v_re[jp * 8 : jp * 8 + 8]
                        a_im = v_im[jp * 8 : jp * 8 + 8]
                        a = u[i] * a_re + u[4 + i] * a_im
                        b = u[4 + i] * a_re - u[i] * a_im
                        n = i * 2 + jp
                        re[n] = a if w == 0 else re[n] + a
                        im[n] = b if w == 0 else im[n] + b
            for n in range(8):
                at = pl.multiple_of(s * 64 + n * 8, 8)
                cross[pl.ds(at, 8), :] = re[n]
                cross[pl.ds(256 + at, 8), :] = im[n]

    def gather(into):
        for h in range(2):
            for k in range(4):
                into[:, h * 512 + k * 128 : h * 512 + (k + 1) * 128] = cross[
                    pl.ds(h * 256 + k, 64, stride=4), :
                ].astype(BF16)

    left_copy = pltpu.make_async_remote_copy(
        src_ref=left_out,
        dst_ref=left.at[1],
        send_sem=peer_send.at[1],
        recv_sem=peer_recv.at[1],
        device_id=peer,
        device_id_type=MESH,
    )
    with jax.named_scope("p06cross"):
        cross_of(other)
        gather(left_out)
        left_copy.start()
        cross_of(c)
        gather(left.at[0])

    with jax.named_scope("p07lag"):
        lagged[...] = jnp.dot(left[0], table[c], preferred_element_type=F32)

        loads[4].wait()
        loads[5].wait()
        row = lax.broadcasted_iota(jnp.int32, (64, 1), 0)
        offset = lax.div(row, 16)
        start = jnp.zeros((64, 1), jnp.int32)
        end = jnp.zeros((64, 1), jnp.int32)
        for s in range(4):
            start = jnp.where(offset == s, starts[0, s], start)
            end = jnp.where(offset == s, ends[0, s], end)
        diagonal = (lax.rem(lax.div(row, 4), 4) == lax.rem(row, 4)) & (offset == 0) & (lay == 0)
        end = jnp.where(diagonal, 0, end)
        left_copy.wait()
        value = lagged[...] + jnp.dot(left[1], table[other], preferred_element_type=F32)
        lag = lax.broadcasted_iota(jnp.int32, (64, 1024), 1)
        keep = (lag >= start) & (lag < end)
        misfit[...] = jnp.where(keep, value - model_rows[...], 0.0).astype(BF16)

    resp_copy = pltpu.make_async_remote_copy(
        src_ref=resp_out,
        dst_ref=resp.at[1],
        send_sem=peer_send.at[2],
        recv_sem=peer_recv.at[2],
        device_id=peer,
        device_id_type=MESH,
    )

    def respond(h, into):
        into[...] = jnp.dot(misfit[...], turned[h], preferred_element_type=F32).astype(BF16)

    def spread(n, t):
        for p in range(2):
            for k in range(4):
                resp_rows[t, pl.ds(p * 256 + k, 64, stride=4), :] = resp[
                    n, :, p * 512 + k * 128 : p * 512 + (k + 1) * 128
                ].astype(F32)

    def terms_of(t):
        @pl.loop(0, 4)
        def _(w):
            at_u = [pl.multiple_of(((p * 4 + w) * 4) * 8, 8) for p in range(2)]
            at_v = [pl.multiple_of((p * 4 + w) * 16, 16) for p in range(2)]
            u = [first[t, pl.ds(at_u[p] + i * 8, 8), :] for p in range(2) for i in range(4)]
            total = [jnp.zeros((8, 128), F32)] * 8
            for s in range(4):
                v = [partner[t + s, pl.ds(at_v[p], 16), :].astype(F32) for p in range(2)]
                for jp in range(2):
                    v_re = v[0][jp * 8 : jp * 8 + 8]
                    v_im = v[1][jp * 8 : jp * 8 + 8]
                    part_re = jnp.zeros((8, 128), F32)
                    part_im = jnp.zeros((8, 128), F32)
                    for i in range(4):
                        at = ((s * 4 + i) * 2 + jp) * 8
                        a = resp_rows[t, at : at + 8, :]
                        b = resp_rows[t, 256 + at : 256 + at + 8, :]
                        total[i] = total[i] + (a * v_re - b * v_im)
                        total[4 + i] = total[4 + i] + (a * v_im + b * v_re)
                        part_re = part_re + (a * u[i] + b * u[4 + i])
                        part_im = part_im + (a * u[4 + i] - b * u[i])
                    part[t, s, pl.ds(at_v[0] + jp * 8, 8), :] = part_re
                    part[t, s, pl.ds(at_v[1] + jp * 8, 8), :] = part_im
            for p in range(2):
                for i in range(4):
                    own[t, pl.ds(((p * 4 + i) * 4 + w) * 8, 8), :] = total[p * 4 + i]

    with jax.named_scope("p08resp"):

        @pl.when(c == 0)
        def _():
            respond(0, resp.at[0])
            respond(1, resp_out)
            resp_copy.start()

        @pl.when(c == 1)
        def _():
            respond(0, resp_out)
            resp_copy.start()
            respond(1, resp.at[0])

        spread(0, c)
        terms_of(c)
        resp_copy.wait()

    with jax.named_scope("p09terms"):
        spread(1, other)
        terms_of(other)

    with jax.named_scope("p10pack"):
        for k in range(4):
            for t in range(2):
                outbox[k, 5 + t] = (
                    own[t, pl.ds(k, 32, stride=8), :] + own[t, pl.ds(4 + k, 32, stride=8), :]
                ).astype(BF16)
            for q in range(5):
                value = [part[t, q - t, pl.ds(k, 32, stride=4), :] for t in range(2) if 0 <= q - t < 4]
                outbox[k, q] = (value[0] if len(value) == 1 else value[0] + value[1]).astype(BF16)

    def across(t):
        to = lax.rem(x + t, 4)
        some = slice(5, 7) if t == 2 else slice(0, 7)
        return pltpu.make_async_remote_copy(
            src_ref=outbox.at[to, some],
            dst_ref=inbox.at[x, some],
            send_sem=x_send,
            recv_sem=x_recv.at[x],
            device_id=(blk, zh * 4 + to),
            device_id_type=MESH,
        )

    def here(n):
        @pl.when(over == n)
        def _():
            pltpu.make_async_copy(inbox.at[n, 5:7], inbox.at[n, 5:7], x_recv.at[n]).wait()

        @pl.when(over != n)
        def _():
            pltpu.make_async_copy(inbox.at[n], inbox.at[n], x_recv.at[n]).wait()

    def straight(q):
        m = 4 * x + q
        slot = lax.div(m, 2) * 2 + zh
        if q == 0:
            slot = jnp.where(x == 0, zh, 20 + zh)
        if q == 4:
            slot = jnp.where(x == 0, 20 + zh, jnp.where(x == 3, 18 + zh, 22 + zh))
        pltpu.make_async_remote_copy(
            src_ref=outbox.at[over, q],
            dst_ref=last.at[slot],
            send_sem=z_send,
            recv_sem=z_recv,
            device_id=(lax.rem(16 * y + 2 * z + m, 64), c * 4 + over),
            device_id_type=MESH,
        ).start()

    def deliver(source, m):
        to, slot = target(m)

        def start():
            pltpu.make_async_remote_copy(
                src_ref=source,
                dst_ref=last.at[slot],
                send_sem=z_send,
                recv_sem=z_recv,
                device_id=to,
                device_id_type=MESH,
            ).start()

        if isinstance(m, int) and m in (0, 17, 18):
            away = elsewhere(to)
            pl.when(away)(start)

            @pl.when(jnp.logical_not(away))
            def _():
                pltpu.make_async_copy(source, last.at[slot], z_recv).start()
        else:
            start()

    with jax.named_scope("p11x"):
        for t in (2, 1, 3):
            across(t).start()
        pltpu.make_async_copy(outbox.at[x], inbox.at[x], x_recv.at[x]).start()
        told(2)

    def merge(n):
        head = jnp.where(over == n, 0.0, inbox[n, 0].astype(F32))
        tail = jnp.where(over == n - 1, 0.0, inbox[n - 1, 4].astype(F32))
        merged[n - 1] = (head + tail).astype(BF16)
        deliver(merged.at[n - 1], 4 * n)

    with jax.named_scope("p12relay"):
        for q in range(5):
            straight(q)
        for q in (3, 2, 1):
            deliver(outbox.at[x, q], 4 * x + q)
        for n, m in ((0, 0), (3, 16)):

            @pl.when(x == n)
            def _():
                deliver(outbox.at[n, m // 4], m)

        for n, single in ((0, (0, 1, 2, 3)), (3, (4, 3, 2, 1)), (1, (3, 2, 1)), (2, (3, 2, 1))):
            here(n)

            @pl.when((x != n) & (over != n))
            def _():
                for q in single:
                    deliver(inbox.at[n, q], 4 * n + q)

            if n == 1:
                merge(1)
        merge(3)
        merge(2)
        for t in range(2):
            value = inbox[0, 5 + t].astype(F32)
            for n in range(1, 4):
                value = value + inbox[n, 5 + t].astype(F32)
            merged[3 + t] = value.astype(BF16)
            deliver(merged.at[3 + t], 17 + t)

    with jax.named_scope("p13wait"):
        for much, now in ((24, (c == 0) & outer), (22, (c == 0) & jnp.logical_not(outer)), (18, c == 1)):

            @pl.when(now)
            def _():
                pltpu.make_async_copy(last.at[0:much], last.at[0:much], z_recv).wait()

    with jax.named_scope("p14sum"):
        total = last[0].astype(F32)
        for n in range(1, 16):
            total = total + last[n].astype(F32)
        scale = 1.0 / 16.0
        raw[32:64, :] = (last[16].astype(F32) + last[17].astype(F32)) * scale

        @pl.when(c == 0)
        def _():
            rest = total
            for n in range(18, 22):
                rest = rest + last[n].astype(F32)
            more = last[22].astype(F32) + last[23].astype(F32)
            raw[0:32, :] = (rest + jnp.where(outer, more, 0.0)) * scale

        @pl.when(c == 1)
        def _():
            raw[0:32, :] = total * scale

        for p in range(2):
            row_of = [
                raw[pl.ds(p * 16 + r, 4, stride=4), :]
                + raw[32 + p * 16 + r * 4 : 32 + p * 16 + r * 4 + 4, :]
                for r in range(4)
            ]
            for q in range(4):
                value = jnp.zeros((4, 128), F32)
                for r in range(4):
                    value = jnp.where(chosen[r][q][:4], row_of[r], value)
                out[p, q] = value

        for half in range(2):

            @pl.when(c == half)
            def _():
                gone = table.at[0, 0 : 96 - 32 * half]
                pltpu.make_async_copy(gone, gone, go_sem).wait()

        gone = table.at[0, 0:64]
        pltpu.make_async_copy(gone, gone, x_send).wait()
        for n in range(18, 22):

            @pl.when(jnp.where(outer, 21, 20) - mine == n)
            def _():
                gone = last.at[0:n]
                pltpu.make_async_copy(gone, gone, z_send).wait()


def local(spectra, model_corr, window_start, window_end, station_slot):
    angles = angle_parts()
    hbm = pl.BlockSpec(memory_space=pl.ANY)
    dma = pltpu.SemaphoreType.DMA
    return pl.pallas_call(
        kernel,
        out_shape=pltpu.VMEM((2, 4, 4, 128), F32),
        in_specs=[hbm] * 6,
        out_specs=pl.BlockSpec(memory_space=pltpu.VMEM),
        scratch_shapes=[
            pltpu.SMEM((1, 4), jnp.int32),
            pltpu.SMEM((1, 4), jnp.int32),
            pltpu.SMEM((1, 4), jnp.int32),
            pltpu.VMEM((2, 4, 4, 1024), BF16),
            pltpu.VMEM((1, 4, 4, 4, 1024), BF16),
            pltpu.VMEM((2, 160, 1024), F32),
            pltpu.VMEM((256, 128), F32),
            pltpu.VMEM((2, 128, 128), F32),
            pltpu.VMEM((2, 128, 128), BF16),
            pltpu.VMEM((128, 128), BF16),
            pltpu.VMEM((2, 256, 128), F32),
            pltpu.VMEM((5, 128, 128), BF16),
            pltpu.VMEM((512, 128), F32),
            pltpu.VMEM((2, 64, 1024), BF16),
            pltpu.VMEM((64, 1024), BF16),
            pltpu.VMEM((2, 1024, 1024), BF16),
            pltpu.VMEM((2, 1024, 1024), BF16),
            pltpu.VMEM((64, 1024), F32),
            pltpu.VMEM((64, 1024), F32),
            pltpu.VMEM((64, 1024), BF16),
            pltpu.VMEM((2, 64, 1024), BF16),
            pltpu.VMEM((64, 1024), BF16),
            pltpu.VMEM((2, 512, 128), F32),
            pltpu.VMEM((2, 256, 128), F32),
            pltpu.VMEM((2, 4, 128, 128), F32),
            pltpu.VMEM((4, 7, 32, 128), BF16),
            pltpu.VMEM((4, 7, 32, 128), BF16),
            pltpu.VMEM((5, 32, 128), BF16),
            pltpu.VMEM((24, 32, 128), BF16),
            dma((6,)), pltpu.SemaphoreType.REGULAR((4,)), dma((3,)), dma((3,)), dma, dma, dma, dma((4,)), dma, dma,
        ],
        compiler_params=pltpu.CompilerParams(has_side_effects=True, collective_id=0),
        name="adjoint",
    )(
        window_start, window_end, station_slot, spectra, model_corr, jnp.asarray(angles),
    )


def solution(mesh):
    in_specs = (
        P(None, "blk", None, None),
        P("blk", "lay", None, None, None),
        P("blk", "lay"),
        P("blk", "lay"),
        P("blk", None),
    )
    out_specs = P(None, "blk", None, "lay")
    return jax.shard_map(local, mesh=mesh, in_specs=in_specs, out_specs=out_specs, check_vma=False)
```
